32 devices in a mesh: sub: 16 (over z, y, core), lm: 2 (over x).
Axes of the slice: x: 2, y: 2, z: 4, core: 2. Of those that a mesh axis runs over, the one named last changes fastest.
Arguments:
- jacobian: bfloat16 [16, 8, 384, 128], P('sub', 'lm'), may hold values from -0.30618622 to 0.30618622
- camera_block: int32 [16, 8], P('sub', 'lm'), may hold values from 0 to 8
- landmark_block: int32 [16, 8], P('sub', 'lm'), may hold values from 9 to 17
Outputs:
- factors: float32 [3, 32, 252, 576], P(None, ('sub', 'lm'))
- top_front: float32 [2, 32, 36, 1152], P(None, ('sub', 'lm'))
The draws below stay inside these ranges and needn't reach their ends.
Inputs may be any that keep to these rules, and one draw needn't show every extreme that they name: `camera_block`: camera parts lie in the first half of a front's unknowns. `landmark_block`: landmark parts lie in the second half of a front's unknowns.
All inputs are finite; a program needn't handle non-finite values.
Results may differ from the reference program's by a relative error of at most 0.0003.
Values may be sent and summed in bfloat16 or wider, within the bound.
No kernel may reach another device: no remote copies, remote signals or barrier semaphores. Data moves between devices by JAX's collectives and lax.ppermute only.
A program may use at most 64 MiB of HBM per device.

```python
import jax
import jax.numpy as jnp
from jax import lax

JR = 384
BW = 64
F = 1152
LEVELS = 3
E = 576
BLOCKS = 8
SUBMAPS = 16
N_LM = 2


def draw_jacobian(key, part):
    shape = (SUBMAPS, BLOCKS, JR, BW)
    first_key = jax.random.fold_in(key, 11)
    second_key = jax.random.fold_in(key, 23)
    camera_cols = jnp.clip(jax.random.normal(first_key, shape, jnp.float32), -3.3, 3.3)
    noise_cols = jnp.clip(jax.random.normal(second_key, shape, jnp.float32), -3.3, 3.3)
    landmark_cols = 0.8 * camera_cols + 0.6 * noise_cols
    scale_value = JR ** (-0.5)
    return (jnp.concatenate([camera_cols, landmark_cols], axis=3) * scale_value).astype(jnp.bfloat16)


def touch_ends(values, key, smallest, high):
    spot = [jax.random.randint(jax.random.fold_in(key, axis), (), 0, length) for axis, length in enumerate(values.shape)]
    widest = values.shape.index(max(values.shape))
    next_to = spot[:widest] + [(spot[widest] + 1) % values.shape[widest]] + spot[widest + 1:]
    return values.at[tuple(spot)].set(smallest).at[tuple(next_to)].set(high)


def setup_inputs(seed: int = 0) -> dict:
    streams_of = jax.random.split(jax.random.key(seed), 4)
    return {
        "jacobian": draw_jacobian(jax.random.fold_in(streams_of[3], 71), 0),
        "camera_block": touch_ends(jax.random.randint(streams_of[1], (SUBMAPS, BLOCKS), 0, F // (2 * BW)), jax.random.fold_in(streams_of[1], 1), 0, (F // (2 * BW)) - 1).astype(jnp.int32),
        "landmark_block": touch_ends(jax.random.randint(streams_of[2], (SUBMAPS, BLOCKS), F // (2 * BW), F // BW), jax.random.fold_in(streams_of[2], 1), F // (2 * BW), (F // BW) - 1).astype(jnp.int32),
    }


damping_value = 1.0

def assemble(blocks, cameras, landmarks):
    block_count = blocks.shape[0]
    widened = blocks.astype(jnp.float32)
    tiles = jnp.einsum('nrc,nrd->ncd', widened, widened, precision=lax.Precision.HIGHEST)
    tiles = tiles.reshape(block_count, 2, BW, 2, BW).transpose(0, 1, 3, 2, 4)
    indices = jnp.stack([cameras, landmarks], axis=1)
    nblocks = F // BW
    blocked = jnp.zeros((nblocks, nblocks, BW, BW), jnp.float32)
    for first in range(2):
        for second in range(2):
            blocked = blocked.at[indices[:, first], indices[:, second]].add(tiles[:, first, second])
    whole_front = blocked.transpose(0, 2, 1, 3).reshape(F, F)
    return whole_front + damping_value * jnp.eye(F, dtype=jnp.float32)

def merge(lower_child, upper_child):
    shared = lower_child[:E, :E] + upper_child[:E, :E]
    diag_factor = jnp.linalg.cholesky(shared)
    coupled = jnp.concatenate([lower_child[E:, :E], upper_child[E:, :E]], axis=0)
    coupling = jax.scipy.linalg.solve_triangular(diag_factor, coupled.T, lower=True).T
    blank = jnp.zeros((E, E), jnp.float32)
    private = jnp.concatenate([jnp.concatenate([lower_child[E:, E:], blank], axis=1), jnp.concatenate([blank, upper_child[E:, E:]], axis=1)], axis=0)
    parent = private - jnp.dot(coupling, coupling.T, precision=lax.Precision.HIGHEST)
    return (diag_factor, coupling, parent)

def cyclic_rows(stacked, spread):
    groups = stacked.shape[0]
    blocks = stacked.shape[1]
    width = stacked.shape[3]
    grouped = stacked.reshape(groups, blocks, E // spread, spread, width)
    return grouped.transpose(1, 0, 3, 2, 4).reshape(blocks, groups * spread, E // spread, width)

def reference(jacobian, camera_block, landmark_block):
    fronts = jax.vmap(assemble)(jacobian, camera_block, landmark_block)
    collected = []
    for depth_level in range(LEVELS):
        diag_factor, coupling, fronts = jax.vmap(merge)(fronts[0::2], fronts[1::2])
        stacked = jnp.concatenate([diag_factor[:, None], coupling.reshape(-1, 2, E, E)], axis=1)
        collected.append(cyclic_rows(stacked, 2 ** (depth_level + 1) * N_LM))
    top_front = cyclic_rows(fronts.reshape(-1, 2, E, F), 2 ** LEVELS * N_LM)
    return (jnp.concatenate(collected, axis=2), top_front)
```

```python
import functools

import jax
import jax.numpy as jnp
from jax import lax
from jax.experimental import pallas as pl
from jax.experimental.pallas import tpu as pltpu
from jax.sharding import PartitionSpec as P

BW = 64
F = 1152
LEVELS = 3
E = 576
NB = E // BW
EP = 640
DAMPING = 1.0
f32 = jnp.float32
bf16 = jnp.bfloat16


def iota(shape, axis):
    return lax.broadcasted_iota(jnp.int32, shape, axis)


def row_of(x, t):
    return jnp.broadcast_to(x[t : t + 1, :], x.shape)


def col_of(x, j):
    return jnp.broadcast_to(x[:, j : j + 1], x.shape)


def split2(x):
    hi = x.astype(bf16)
    return hi, (x - hi.astype(f32)).astype(bf16)


def left4(dup):
    hi, lo = split2(dup)
    return jnp.concatenate([hi, lo], axis=1)


def right4(x):
    hi, lo = split2(x)
    return jnp.concatenate([hi, lo, hi, lo], axis=0)


def dot(a, b):
    return jnp.dot(a, b, preferred_element_type=f32)


def dot_nt(a, b):
    return lax.dot_general(a, b, (((1,), (1,)), ((), ())), preferred_element_type=f32)


def roll64(x):
    return pltpu.roll(x, 64, 1)


def factor(mats, ahead):
    sub = iota((8, 128), 0)
    for kb in range(8):
        live = 8 - kb
        cols = None
        if ahead:
            cols = [[[col_of(m[v], 8 * kb + t) for v in range(kb, 8)] for t in range(8)] for m in mats]
        diag = [jnp.ones((8, 128), f32) for _ in mats]
        for t in range(8):
            for b, m in enumerate(mats):
                if ahead:
                    col = cols[b][t]
                else:
                    col = [col_of(m[v], 8 * kb + t) for v in range(kb, 8)]
                d = row_of(col[0], t)
                rd = 1.0 / d
                diag[b] = jnp.where(sub == t, d, diag[b])
                pivot = row_of(m[kb], t)
                mult = [x * rd for x in col]
                mult[0] = jnp.where(sub > t, mult[0], 0.0)
                if ahead:
                    for t2 in range(t + 1, 8):
                        s = row_of(col[0], t2)
                        for v in range(live):
                            cols[b][t2][v] = cols[b][t2][v] - mult[v] * s
                for v in range(live):
                    m[kb + v] = m[kb + v] - mult[v] * pivot
        for b, m in enumerate(mats):
            m[kb] = m[kb] * lax.rsqrt(diag[b])
    return mats


def augmented(x):
    lane, row = iota((64, 128), 1), iota((64, 128), 0)
    full = jnp.where(lane < 64, x, jnp.where(lane - 64 == row, 1.0, 0.0))
    return [full[8 * v : 8 * v + 8] for v in range(8)]


def joined(rows):
    return jnp.concatenate(rows, axis=0)


def tiles_kernel(cam_ref, jac_ref, pay_ref, sum_ref):
    lane = iota((64, 128), 1)
    sum_ref[...] = jnp.zeros_like(sum_ref)
    for n in range(jac_ref.shape[0]):
        j = jac_ref[n]
        t = lax.dot_general(j, j, (((0,), (0,)), ((), ())), preferred_element_type=f32)
        top, bottom = t[:64], t[64:]
        pay_ref[n] = jnp.where(lane < 64, roll64(top), bottom)
        c = cam_ref[n]
        cc = jnp.where(lane < 64, top, roll64(top))
        mine = (lane >= 64).astype(jnp.int32) == c % 2
        at = pl.ds(pl.multiple_of(c // 2 * 64, 64), 64)
        sum_ref[at, :] = sum_ref[at, :] + jnp.where(mine, cc, 0.0)


def bottom_kernel(info_ref, cam_ref, sum_a, sum_b, pay_ref, out_ref, own_ref, w_ref):
    lane, row = iota((64, 128), 1), iota((64, 128), 0)
    own_ref[...] = jnp.zeros_like(own_ref)
    mats = []
    for c in range(NB):
        at = slice(c // 2 * 64, c // 2 * 64 + 64)
        x = sum_a[at, :] + sum_b[at, :]
        if c % 2:
            x = roll64(x)
        mats.append(augmented(x + jnp.where(lane == row, 2 * DAMPING, 0.0)))
    mats = factor(mats, False)
    spread = info_ref[4]
    place = info_ref[1]
    count = own_ref.shape[0] // NB
    pick = (iota((count, 128), 1) == iota((count, 128), 0) * spread + place).astype(bf16)
    for c in range(NB):
        v = joined(mats[c])
        w = roll64(v)
        w_ref[c] = left4(jnp.where(lane < 64, w, v))
        upper = jnp.where((lane >= row) & (lane < 64), v, 0.0)
        hi, lo = split2(upper)
        got = dot_nt(pick, hi) + dot_nt(pick, lo)
        own_ref[count * c : count * c + count, 64 * c : 64 * c + 64] = got
    for n in range(pay_ref.shape[0]):
        x = pay_ref[n]
        cl = jnp.where(lane < 64, x, roll64(x))
        y = dot(w_ref[cam_ref[n]], right4(cl))
        out_ref[n] = jnp.where(lane < 64, y, x)


def climb(a_ref, batch):
    width = a_ref.shape[2]
    lane64, row64 = iota((64, 128), 1), iota((64, 128), 0)
    cuts = (0, 3, 6, 9)

    for first, last in zip(cuts[:-1], cuts[1:]):
        low_row = 64 * first
        low_lane = low_row // 128 * 128
        chunk = 640
        starts = [low_lane] + list(range(640, width, chunk))
        sizes = [640 - low_lane] + [chunk] * (len(starts) - 1)

        def step(j, carry, low_row=low_row, starts=starts, sizes=sizes):
            at = pl.ds(pl.multiple_of(j * 64, 64), 64)
            wide = pl.ds(pl.multiple_of(j // 2 * 128, 128), 128)
            odd = j % 2 == 1
            mats = []
            for b in range(batch):
                x = a_ref[b, at, wide]
                mats.append(augmented(jnp.where(odd, roll64(x), x)))
            mats = factor(mats, True)
            for b in range(batch):
                v = joined(mats[b])
                w4 = left4(jnp.where(lane64 < 64, roll64(v), v))
                u = dot(w4, right4(a_ref[b, at, :]))
                keep = iota((64, width), 1) >= j * 64 + iota((64, width), 0)
                u = jnp.where(keep, u, 0.0)
                a_ref[b, at, :] = u
                beyond = iota((64, EP), 1) >= j * 64 + 64
                xs = jnp.where(beyond, -u[:, :EP], 0.0)
                xt = jnp.concatenate([xs, xs], axis=0).T
                left = left4(xt[low_row:E])
                for s, size in zip(starts, sizes):
                    r = right4(u[:, s : s + size])
                    a_ref[b, low_row:E, s : s + size] = a_ref[b, low_row:E, s : s + size] + dot(left, r)
            return carry

        lax.fori_loop(first, last, step, 0)


def gram_setup(u, left_ref, right_ref, first):
    hi, lo = split2(u)
    right_ref[0:EP] = hi
    right_ref[EP : 2 * EP] = lo
    right_ref[2 * EP :] = hi


def gram_left(u, left_ref):
    xt = (-u).T
    hi, lo = split2(xt)
    left_ref[:, 0:EP] = hi
    left_ref[:, EP : 2 * EP] = hi
    left_ref[:, 2 * EP :] = lo


def picked(pick, u):
    hi, lo = split2(u)
    return dot_nt(pick, hi) + dot_nt(pick, lo)


def upper_kernel(nslots, info_ref, cam_ref, lm_ref, *refs):
    pays = refs[:nslots]
    own0_ref, fac_ref, top_ref = refs[nslots : nslots + 3]
    u0, a1, a2, pri, left_ref, right_ref = refs[nslots + 3 :]
    lane = iota((64, 128), 1)
    me = info_ref[0]
    blocks = pays[0].shape[0]

    eye2 = jnp.where(iota((E, EP), 0) == iota((E, EP), 1), 2 * DAMPING, 0.0)
    u0[...] = jnp.zeros_like(u0)
    a1[...] = jnp.zeros_like(a1)
    a2[...] = jnp.zeros_like(a2)
    for m in range(2):
        a1[m, 0:E, 0:EP] = eye2
        pri[m] = 0.5 * eye2
    a2[0, 0:E, 0:EP] = eye2

    for slot in range(nslots):
        s = me ^ (slot // 2)
        pair = s // 2
        half = s % 2
        merge = s // 4
        second = pair % 2
        for n in range(blocks):
            c = cam_ref[slot * blocks + n]
            l = lm_ref[slot * blocks + n]
            x = pays[slot][n]
            xr = roll64(x)
            mine = (lane >= 64).astype(jnp.int32) == l % 2
            y = jnp.where(mine, jnp.where(lane < 64, x, xr), 0.0)
            ll = jnp.where(mine, jnp.where(lane < 64, xr, x), 0.0)
            crows = pl.ds(pl.multiple_of(c * 64, 64), 64)
            lrows = pl.ds(pl.multiple_of(l * 64, 64), 64)
            lanes = pl.ds(pl.multiple_of(half * EP + l // 2 * 128, 128), 128)
            llanes = pl.ds(pl.multiple_of(l // 2 * 128, 128), 128)
            u0[pair, crows, lanes] = u0[pair, crows, lanes] + y

            @pl.when(half == 0)
            def _():
                a1[merge, lrows, llanes] = a1[merge, lrows, llanes] + ll

            @pl.when((half == 1) & (second == 0))
            def _():
                a2[0, lrows, llanes] = a2[0, lrows, llanes] + ll

            @pl.when((half == 1) & (second == 1))
            def _():
                pri[merge, lrows, llanes] = pri[merge, lrows, llanes] + ll

    def gram_pair(p, carry):
        m = p // 2
        gram_setup(u0[p], left_ref, right_ref, 0)
        gram_left(u0[p, :, 0:EP], left_ref)
        a1[m, 0:E, 0:EP] = a1[m, 0:E, 0:EP] + dot(left_ref[0:E], right_ref[:, 0:EP])
        to = pl.ds(pl.multiple_of(EP + p % 2 * EP, 128), EP)
        a1[m, 0:E, to] = dot(left_ref[0:E], right_ref[:, EP : 2 * EP])

        @pl.when(p % 2 == 0)
        def _():
            gram_left(u0[p, :, EP : 2 * EP], left_ref)
            a2[0, 0:E, 0:EP] = a2[0, 0:E, 0:EP] + dot(left_ref[0:E], right_ref[:, EP : 2 * EP])

        return carry

    lax.fori_loop(0, 4, gram_pair, 0)

    climb(a1, 2)

    def gram_merge(m, carry):
        u = a1[m, :, EP : 3 * EP]
        gram_setup(u, left_ref, right_ref, 0)
        gram_left(u[:, 0:EP], left_ref)
        a2[0, 0:E, 0:EP] = a2[0, 0:E, 0:EP] + dot(left_ref[0:E], right_ref[:, 0:EP])
        to = pl.ds(pl.multiple_of(EP + m * EP, 128), EP)
        a2[0, 0:E, to] = dot(left_ref[0:E], right_ref[:, EP : 2 * EP])
        return carry

    lax.fori_loop(0, 2, gram_merge, 0)

    climb(a2, 1)

    def pick_of(count, spread, place):
        return (iota((count, EP), 1) == iota((count, EP), 0) * spread + place).astype(bf16)

    lm_count = info_ref[4] // 2
    n0, n1, n2 = own0_ref.shape[0], own0_ref.shape[0] // 2, own0_ref.shape[0] // 4
    fac_ref[0, 0:n0, :] = own0_ref[...]
    pair = me // 2
    merge = me // 4
    pick0 = pick_of(n0, 2 * lm_count, info_ref[1])
    pick1 = pick_of(n1, 4 * lm_count, info_ref[2])
    pick2 = pick_of(n2, 8 * lm_count, info_ref[3])
    fac_ref[1, 0:n0, :] = picked(pick0, u0[pair, 0:E, 0:EP])
    fac_ref[2, 0:n0, :] = picked(pick0, u0[pair, 0:E, EP : 2 * EP])
    for t in range(3):
        fac_ref[t, n0 : n0 + n1, :] = picked(pick1, a1[merge, 0:E, t * EP : t * EP + EP])
    for t in range(3):
        fac_ref[t, n0 + n1 : n0 + n1 + n2, :] = picked(pick2, a2[0, 0:E, t * EP : t * EP + EP])

    def minus_rows(rows, u):
        hi, lo = split2(-rows)
        uh, ul = split2(u)
        return dot(hi, uh) + dot(hi, ul) + dot(lo, uh)

    for h in range(2):
        u0up = u0[2 * h + 1, 0:E, EP : 2 * EP]
        u1up = a1[h, 0:E, 2 * EP : 3 * EP]
        hi, lo = split2(pri[h])
        own = dot(pick2[:, 0:E], hi) + dot(pick2[:, 0:E], lo)
        own = own + minus_rows(picked(pick2, u0up), u0up)
        own = own + minus_rows(picked(pick2, u1up), u1up)
        rows = fac_ref[1 + h, n0 + n1 : n0 + n1 + n2, :]
        for g in range(2):
            part = minus_rows(rows, a2[0, 0:E, (1 + g) * EP : (2 + g) * EP])
            if g == h:
                part = part + own
            top_ref[h, :, g * E : g * E + E] = part[:, 0:E]


def vmem(n):
    return [pl.BlockSpec(memory_space=pltpu.VMEM)] * n


def smem(n):
    return [pl.BlockSpec(memory_space=pltpu.SMEM)] * n


LIMIT = 60 * 1024 * 1024


def local(jacobian, camera_block, landmark_block):
    lm_count = lax.axis_size("lm")
    sub_count = lax.axis_size("sub")
    lm_place = lax.axis_index("lm")
    sub_place = lax.axis_index("sub")
    group = 2**LEVELS
    jac = jacobian[0]
    blocks = jac.shape[0]

    def swap(value, sub_mask, lm_mask):
        pairs = [
            (s * lm_count + l, (s ^ sub_mask) * lm_count + (l ^ lm_mask))
            for s in range(sub_count)
            for l in range(lm_count)
        ]
        return lax.ppermute(value, ("sub", "lm"), pairs)

    info = jnp.stack(
        [
            sub_place % group,
            sub_place % 2 * lm_count + lm_place,
            sub_place % 4 * lm_count + lm_place,
            sub_place % 8 * lm_count + lm_place,
            jnp.int32(2 * lm_count),
        ]
    ).astype(jnp.int32)
    cams = camera_block[0]
    lms = landmark_block[0] - NB

    pay, sums = pl.pallas_call(
        tiles_kernel,
        out_shape=(
            jax.ShapeDtypeStruct((blocks, 64, 128), f32),
            jax.ShapeDtypeStruct(((NB + 1) // 2 * 64, 128), f32),
        ),
        in_specs=smem(1) + vmem(1),
        out_specs=tuple(vmem(2)),
    )(cams, jac)
    half_sums = sums + swap(sums, 1, 0)
    other_sums = swap(half_sums, 0, 1)

    count0 = E // (2 * lm_count)
    pay, own0 = pl.pallas_call(
        bottom_kernel,
        out_shape=(
            jax.ShapeDtypeStruct((blocks, 64, 128), f32),
            jax.ShapeDtypeStruct((count0, E), f32),
        ),
        in_specs=smem(2) + vmem(3),
        out_specs=tuple(vmem(2)),
        scratch_shapes=[pltpu.VMEM((NB, 64, 256), bf16)],
    )(info, cams, half_sums, other_sums, pay)

    def gather(value):
        slots = [value]
        slots = slots + [swap(v, 0, 1) for v in slots]
        for mask in (2, 4, 1):
            slots = slots + [swap(v, mask, 0) for v in slots]
        order = {}
        keys = [(0, 0), (0, 1)]
        for mask in (2, 4, 1):
            keys = keys + [(q ^ mask, l) for q, l in keys]
        for key, v in zip(keys, slots):
            order[key] = v
        return [order[q, l] for q in range(group) for l in range(2)]

    slots = gather(pay)
    index = jnp.stack([cams, lms])
    index_slots = jnp.stack(gather(index), axis=1)
    nslots = len(slots)
    factors, top = pl.pallas_call(
        functools.partial(upper_kernel, nslots),
        out_shape=(
            jax.ShapeDtypeStruct((3, count0 * 7 // 4, E), f32),
            jax.ShapeDtypeStruct((2, count0 // 4, F), f32),
        ),
        in_specs=smem(3) + vmem(nslots + 1),
        out_specs=tuple(vmem(2)),
        scratch_shapes=[
            pltpu.VMEM((4, EP, 2 * EP), f32),
            pltpu.VMEM((2, EP, 3 * EP), f32),
            pltpu.VMEM((1, EP, 3 * EP), f32),
            pltpu.VMEM((2, E, EP), f32),
            pltpu.VMEM((EP, 3 * EP), bf16),
            pltpu.VMEM((3 * EP, 2 * EP), bf16),
        ],
        compiler_params=pltpu.CompilerParams(vmem_limit_bytes=LIMIT),
    )(info, index_slots[0].reshape(-1), index_slots[1].reshape(-1), *slots, own0)
    return factors[:, None], top[:, None]


def solution(mesh):
    placed = (P("sub", "lm", None, None), P("sub", "lm"), P("sub", "lm"))
    return jax.shard_map(
        local,
        mesh=mesh,
        in_specs=placed,
        out_specs=(P(None, ("sub", "lm"), None, None), P(None, ("sub", "lm"), None, None)),
        check_vma=False,
    )
```

```python
import functools

import jax
import jax.numpy as jnp
from jax import lax
from jax.experimental import pallas as pl
from jax.experimental.pallas import tpu as pltpu
from jax.sharding import PartitionSpec as P

BW = 64
F = 1152
LEVELS = 3
E = 576
NB = E // BW
EP = 640
DAMPING = 1.0
f32 = jnp.float32
bf16 = jnp.bfloat16


def iota(shape, axis):
    return lax.broadcasted_iota(jnp.int32, shape, axis)


def row_of(x, t):
    return jnp.broadcast_to(x[t : t + 1, :], x.shape)


def col_of(x, j):
    return jnp.broadcast_to(x[:, j : j + 1], x.shape)


def split2(x):
    hi = x.astype(bf16)
    return hi, (x - hi.astype(f32)).astype(bf16)


def left4(dup):
    hi, lo = split2(dup)
    return jnp.concatenate([hi, lo], axis=1)


def right4(x):
    hi, lo = split2(x)
    return jnp.concatenate([hi, lo, hi, lo], axis=0)


def dot(a, b):
    return jnp.dot(a, b, preferred_element_type=f32)


def dot_nt(a, b):
    return lax.dot_general(a, b, (((1,), (1,)), ((), ())), preferred_element_type=f32)


def roll64(x):
    return pltpu.roll(x, 64, 1)


def factor(mats):
    sub = iota((8, 128), 0)
    for kb in range(8):
        state = []
        for m in mats:
            x = m[kb]
            cols = [col_of(x, 8 * kb + t) for t in range(8)]
            state.append([x, x, cols, jnp.ones((8, 128), f32), jnp.ones((8, 128), f32)])
        below = [
            [[col_of(m[v], 8 * kb + t) for t in range(8)] for v in range(kb + 1, 8)] for m in mats
        ]
        for t in range(8):
            for st in state:
                fwd, both, cols, diag, recip = st
                col = cols[t]
                d = row_of(col, t)
                rd = 1.0 / d
                st[3] = jnp.where(sub == t, d, diag)
                st[4] = jnp.where(sub == t, rd, recip)
                mult = jnp.where(sub == t, 0.0, col * rd)
                for t2 in range(t + 1, 8):
                    cols[t2] = cols[t2] - mult * row_of(cols[t2], t)
                st[1] = both - mult * row_of(both, t)
                st[0] = fwd - jnp.where(sub > t, mult, 0.0) * row_of(fwd, t)
        for b, m in enumerate(mats):
            fwd, both, cols, diag, recip = state[b]
            m[kb] = fwd * lax.rsqrt(diag)
            solved = both * recip
            rows = [row_of(solved, t) for t in range(8)]
            for v in range(kb + 1, 8):
                acc = None
                for t in range(8):
                    term = below[b][v - kb - 1][t] * rows[t]
                    acc = term if acc is None else acc + term
                m[v] = m[v] - acc
    return mats


def augmented(x):
    lane, row = iota((64, 128), 1), iota((64, 128), 0)
    full = jnp.where(lane < 64, x, jnp.where(lane - 64 == row, 1.0, 0.0))
    return [full[8 * v : 8 * v + 8] for v in range(8)]


def joined(rows):
    return jnp.concatenate(rows, axis=0)


def tiles_kernel(cam_ref, lm_ref, jac_ref, pay_ref, sum_ref):
    lane = iota((64, 128), 1)
    blocks = jac_ref.shape[0]
    sum_ref[...] = jnp.zeros_like(sum_ref)
    lane8, row8 = iota((8, 128), 1), iota((8, 128), 0)
    index = jnp.zeros((8, 128), f32)
    for n in range(blocks):
        j = jac_ref[n]
        t = lax.dot_general(j, j, (((0,), (0,)), ((), ())), preferred_element_type=f32)
        top, bottom = t[:64], t[64:]
        pay_ref[64 * n : 64 * n + 64, :] = jnp.where(lane < 64, roll64(top), bottom)
        c = cam_ref[n]
        cc = jnp.where(lane < 64, top, roll64(top))
        mine = (lane >= 64).astype(jnp.int32) == c % 2
        at = pl.ds(pl.multiple_of(c // 2 * 64, 64), 64)
        sum_ref[at, :] = sum_ref[at, :] + jnp.where(mine, cc, 0.0)
        index = jnp.where((lane8 == n) & (row8 == 0), c.astype(f32), index)
        index = jnp.where((lane8 == n) & (row8 == 1), lm_ref[n].astype(f32), index)
    pay_ref[64 * blocks :, :] = index


def bottom_kernel(info_ref, cam_ref, sum_a, sum_b, pay_ref, out_ref, own_ref, w_ref):
    lane, row = iota((64, 128), 1), iota((64, 128), 0)
    own_ref[...] = jnp.zeros_like(own_ref)
    mats = []
    for c in range(NB):
        at = slice(c // 2 * 64, c // 2 * 64 + 64)
        x = sum_a[at, :] + sum_b[at, :]
        if c % 2:
            x = roll64(x)
        mats.append(augmented(x + jnp.where(lane == row, 2 * DAMPING, 0.0)))
    mats = factor(mats)
    spread = info_ref[4]
    place = info_ref[1]
    count = own_ref.shape[1] // NB
    pick = (iota((128, count), 0) == iota((128, count), 1) * spread + place).astype(bf16)
    for c in range(NB):
        v = joined(mats[c])
        w = roll64(v)
        w_ref[c] = left4(jnp.where(lane < 64, w, v))
        upper = jnp.where((lane >= row) & (lane < 64), v, 0.0)
        hi, lo = split2(upper)
        own_ref[64 * c : 64 * c + 64, count * c : count * c + count] = dot(hi, pick) + dot(lo, pick)
    blocks = cam_ref.shape[0]
    for n in range(blocks):
        x = pay_ref[64 * n : 64 * n + 64, :]
        cl = jnp.where(lane < 64, x, roll64(x))
        y = dot(w_ref[cam_ref[n]], right4(cl))
        out_ref[64 * n : 64 * n + 64, :] = jnp.where(lane < 64, y, x)
    out_ref[64 * blocks :, :] = pay_ref[64 * blocks :, :]


def climb(a_ref, d_ref, l_ref, r_ref, batch):
    width = a_ref.shape[2]
    lane64 = iota((64, 128), 1)
    cuts = (0, 3, 6, 9)
    for b in range(batch):
        d_ref[b] = a_ref[b, 0:64, 0:128]
        l_ref[b] = jnp.zeros(l_ref.shape[1:], bf16)
        r_ref[b] = jnp.zeros(r_ref.shape[1:], bf16)

    for first, last in zip(cuts[:-1], cuts[1:]):
        low_row = 64 * first
        low_lane = low_row // 128 * 128
        starts = [low_lane] + list(range(EP, width, EP))
        sizes = [EP - low_lane] + [EP] * (len(starts) - 1)

        def step(j, carry, low_row=low_row, starts=starts, sizes=sizes):
            at = pl.ds(pl.multiple_of(j * 64, 64), 64)
            mats = factor([augmented(d_ref[b]) for b in range(batch)])
            for b in range(batch):
                left = l_ref[b, low_row:E]
                for s, size in zip(starts, sizes):
                    a_ref[b, low_row:E, s : s + size] = a_ref[b, low_row:E, s : s + size] + dot(
                        left, r_ref[b, :, s : s + size]
                    )
            after = j + 1
            rows = pl.ds(pl.multiple_of(after * 64, 64), 64)
            wide = pl.ds(pl.multiple_of(after // 2 * 128, 128), 128)
            for b in range(batch):
                v = joined(mats[b])
                w4 = left4(jnp.where(lane64 < 64, roll64(v), v))
                u = dot(w4, right4(a_ref[b, at, :]))
                keep = iota((64, width), 1) >= j * 64 + iota((64, width), 0)
                u = jnp.where(keep, u, 0.0)
                a_ref[b, at, :] = u
                beyond = iota((64, EP), 1) >= j * 64 + 64
                xs = jnp.where(beyond, -u[:, :EP], 0.0)
                l_ref[b] = left4(jnp.concatenate([xs, xs], axis=0).T)
                r_ref[b] = right4(u)
                x = a_ref[b, rows, wide] + dot(l_ref[b, rows, :], r_ref[b, :, wide])
                d_ref[b] = jnp.where(after % 2 == 1, roll64(x), x)
            return carry

        lax.fori_loop(first, last, step, 0)


def gram_left(u, left_ref):
    hi, lo = split2((-u).T)
    left_ref[:, 0:EP] = hi
    left_ref[:, EP : 2 * EP] = hi
    left_ref[:, 2 * EP :] = lo


def picked(pick, u):
    hi, lo = split2(u)
    return dot_nt(pick, hi) + dot_nt(pick, lo)


def spread_lanes(pick, u):
    hi, lo = split2(u)
    return dot(hi, pick) + dot(lo, pick)


def minus_rows(rows, u):
    hi, lo = split2(-rows)
    uh, ul = split2(u)
    return dot(hi, uh) + dot(hi, ul) + dot(lo, uh)


def upper_kernel(nslots, blocks, info_ref, *refs):
    pays = refs[:nslots]
    own0_ref, fac_ref, top_ref = refs[nslots : nslots + 3]
    (all_ref, ivm, ism, sem, ydup, tbuf, lbuf, own_u0, odd_up, a1, a2, pri) = refs[nslots + 3 : nslots + 15]
    (d_ref, l_ref, r_ref, left_ref, right_ref) = refs[nslots + 15 :]
    lane = iota((64, 128), 1)
    me, my_lm = info_ref[0], info_ref[5]
    lm_count = info_ref[4] // 2
    per = blocks * nslots // 8

    for slot in range(nslots):
        s = me ^ (slot // 2)
        spot = s * 2 + (my_lm ^ (slot % 2))
        at = pl.ds(pl.multiple_of(spot * blocks * 64, 64), blocks * 64)
        all_ref[at, :] = pays[slot][0 : 64 * blocks, :]
        ivm[pl.ds(pl.multiple_of(spot * 8, 8), 8), :] = pays[slot][64 * blocks :, :].astype(jnp.int32)
    copy = pltpu.make_async_copy(ivm, ism, sem)
    copy.start()
    eye2 = jnp.where(iota((E, EP), 0) == iota((E, EP), 1), 2 * DAMPING, 0.0)
    own_u0[...] = jnp.zeros_like(own_u0)
    odd_up[...] = jnp.zeros_like(odd_up)
    for m in range(2):
        a1[m] = jnp.zeros(a1.shape[1:], f32)
        a1[m, 0:E, 0:EP] = eye2
        pri[m] = 0.5 * eye2
    a2[0] = jnp.zeros(a2.shape[1:], f32)
    a2[0, 0:E, 0:EP] = eye2
    copy.wait()

    def ids(s, k):
        row = (s * 2 + k // blocks) * 8
        return ism[row, k % blocks], ism[row + 1, k % blocks]

    def rows64(i):
        return pl.ds(pl.multiple_of(i * 64, 64), 64)

    def lanes128(i):
        return pl.ds(pl.multiple_of(i * 128, 128), 128)

    def dups(s, k):
        x = all_ref[rows64(s * per + k), :]
        xr = roll64(x)
        return jnp.where(lane < 64, x, xr), jnp.where(lane < 64, xr, x)

    def half_of(l):
        return (lane >= 64).astype(jnp.int32) == l % 2

    for s in range(8):
        pair, half, merge = s // 2, s % 2, s // 4
        second = pair % 2

        def place(k, carry, s=s, pair=pair, half=half, merge=merge, second=second):
            c, l = ids(s, k)
            y, ll = dups(s, k)
            mine = half_of(l)
            ydup[pair, :, lanes128(half * per + k)] = y
            rows, lanes = rows64(l), lanes128(l // 2)
            ll = jnp.where(mine, ll, 0.0)
            if half == 0:
                a1[merge, rows, lanes] = a1[merge, rows, lanes] + ll
            elif second == 0:
                a2[0, rows, lanes] = a2[0, rows, lanes] + ll
            else:
                pri[merge, rows, lanes] = pri[merge, rows, lanes] + ll
                odd_up[merge, rows64(c), lanes] = odd_up[merge, rows64(c), lanes] + jnp.where(mine, y, 0.0)
            return carry

        lax.fori_loop(0, per, place, 0)

    my_pair = me // 2
    for half in range(2):

        def place_own(k, carry, half=half):
            c, l = ids(2 * my_pair + half, k)
            y, _ = dups(2 * my_pair + half, k)
            lanes = lanes128(half * (EP // 128) + l // 2)
            own_u0[rows64(c), lanes] = own_u0[rows64(c), lanes] + jnp.where(half_of(l), y, 0.0)
            return carry

        lax.fori_loop(0, per, place_own, 0)

    def gram_pair(p, carry):
        merge = p // 2

        def transposed(first):
            for k in range(per):
                t = ydup[p, :, 128 * (first + k) : 128 * (first + k + 1)]
                tt = jnp.concatenate([t, t], axis=0).T
                lbuf[64 * k : 64 * k + 64, :] = left4(-tt[0:64])

        def scatter(target, s_rows, halves, base):
            def body(n, carry):
                cn, ln = ids(s_rows, n)
                for i, h in enumerate(halves):
                    for k in range(per):
                        ck, lk = ids(2 * p + h, k)

                        @pl.when(ck == cn)
                        def _():
                            got = tbuf[rows64(n), 128 * (i * per + k) : 128 * (i * per + k + 1)]
                            to = pl.ds(pl.multiple_of(base[h] + lk // 2 * 128, 128), 128)
                            view = target.at[rows64(ln), to]
                            view[...] = view[...] + jnp.where(half_of(lk), got, 0.0)

                return carry

            lax.fori_loop(0, per, body, 0)

        transposed(0)
        wide = 128 * per
        for h in range(2):
            tbuf[:, h * wide : h * wide + wide] = dot(lbuf[...], right4(ydup[p, :, h * wide : h * wide + wide]))
        scatter(a1.at[merge], 2 * p, (0, 1), (0, EP + p % 2 * EP))

        @pl.when(p % 2 == 0)
        def _():
            transposed(per)
            tbuf[:, 0:wide] = dot(lbuf[...], right4(ydup[p, :, wide : 2 * wide]))
            scatter(a2.at[0], 2 * p + 1, (1,), (0, 0))

        return carry

    lax.fori_loop(0, 4, gram_pair, 0)

    climb(a1, d_ref, l_ref, r_ref, 2)

    def gram_merge(m, carry):
        u = a1[m, :, EP : 3 * EP]
        hi, lo = split2(u)
        right_ref[0:EP] = hi
        right_ref[EP : 2 * EP] = lo
        right_ref[2 * EP :] = hi
        gram_left(u[:, 0:EP], left_ref)
        a2[0, 0:E, 0:EP] = a2[0, 0:E, 0:EP] + dot(left_ref[0:E], right_ref[:, 0:EP])
        to = pl.ds(pl.multiple_of(EP + m * EP, 128), EP)
        a2[0, 0:E, to] = dot(left_ref[0:E], right_ref[:, EP : 2 * EP])
        return carry

    lax.fori_loop(0, 2, gram_merge, 0)

    climb(a2, d_ref, l_ref, r_ref, 1)

    def pick_of(count, spread, place):
        return (iota((EP, count), 0) == iota((EP, count), 1) * spread + place).astype(bf16)

    n0 = own0_ref.shape[1]
    n1, n2 = n0 // 2, n0 // 4
    merge = me // 4
    pick0 = pick_of(n0, 2 * lm_count, info_ref[1])
    pick1 = pick_of(n1, 4 * lm_count, info_ref[2])
    pick2 = pick_of(n2, 8 * lm_count, info_ref[3])
    fac_ref[0, :, 0:n0] = own0_ref[...]
    fac_ref[1, :, 0:n0] = spread_lanes(pick0, own_u0[:, 0:EP])
    fac_ref[2, :, 0:n0] = spread_lanes(pick0, own_u0[:, EP : 2 * EP])
    for t in range(3):
        fac_ref[t, :, n0 : n0 + n1] = spread_lanes(pick1, a1[merge, 0:E, t * EP : t * EP + EP])
    for t in range(3):
        fac_ref[t, :, n0 + n1 : n0 + n1 + n2] = spread_lanes(pick2, a2[0, 0:E, t * EP : t * EP + EP])

    pick = (iota((n2, EP), 1) == iota((n2, EP), 0) * (8 * lm_count) + info_ref[3]).astype(bf16)
    for h in range(2):
        u0up = odd_up[h]
        u1up = a1[h, 0:E, 2 * EP : 3 * EP]
        hi, lo = split2(pri[h])
        own = dot(pick[:, 0:E], hi) + dot(pick[:, 0:E], lo)
        own = own + minus_rows(picked(pick, u0up), u0up)
        own = own + minus_rows(picked(pick, u1up), u1up)
        rows = picked(pick, a2[0, 0:E, (1 + h) * EP : (2 + h) * EP])
        for g in range(2):
            part = minus_rows(rows, a2[0, 0:E, (1 + g) * EP : (2 + g) * EP])
            if g == h:
                part = part + own
            top_ref[h, :, g * E : g * E + E] = part[:, 0:E]


def vmem(n):
    return [pl.BlockSpec(memory_space=pltpu.VMEM)] * n


def smem(n):
    return [pl.BlockSpec(memory_space=pltpu.SMEM)] * n


LIMIT = 60 * 1024 * 1024


def local(jacobian, camera_block, landmark_block):
    lm_count = lax.axis_size("lm")
    sub_count = lax.axis_size("sub")
    lm_place = lax.axis_index("lm")
    sub_place = lax.axis_index("sub")
    group = 2**LEVELS
    jac = jacobian[0]
    blocks = jac.shape[0]

    def swap(value, sub_mask, lm_mask):
        pairs = [
            (s * lm_count + l, (s ^ sub_mask) * lm_count + (l ^ lm_mask))
            for s in range(sub_count)
            for l in range(lm_count)
        ]
        return lax.ppermute(value, ("sub", "lm"), pairs)

    info = jnp.stack(
        [
            sub_place % group,
            sub_place % 2 * lm_count + lm_place,
            sub_place % 4 * lm_count + lm_place,
            sub_place % 8 * lm_count + lm_place,
            jnp.int32(2 * lm_count),
            lm_place,
        ]
    ).astype(jnp.int32)
    cams = camera_block[0]
    lms = landmark_block[0] - NB
    payload = jax.ShapeDtypeStruct((64 * blocks + 8, 128), f32)

    pay, sums = pl.pallas_call(
        tiles_kernel,
        out_shape=(payload, jax.ShapeDtypeStruct(((NB + 1) // 2 * 64, 128), f32)),
        in_specs=smem(2) + vmem(1),
        out_specs=tuple(vmem(2)),
    )(cams, lms, jac)
    half_sums = sums + swap(sums, 1, 0)
    other_sums = swap(half_sums, 0, 1)

    count0 = E // (2 * lm_count)
    pay, own0 = pl.pallas_call(
        bottom_kernel,
        out_shape=(payload, jax.ShapeDtypeStruct((E, count0), f32)),
        in_specs=smem(2) + vmem(3),
        out_specs=tuple(vmem(2)),
        scratch_shapes=[pltpu.VMEM((NB, 64, 256), bf16)],
    )(info, cams, half_sums, other_sums, pay)

    held = {(0, 0): pay}
    for sub_mask, lm_mask in ((0, 1), (2, 0), (4, 0), (1, 0)):
        held.update({(q ^ sub_mask, l ^ lm_mask): swap(v, sub_mask, lm_mask) for (q, l), v in held.items()})
    slots = [held[q, l] for q in range(group) for l in range(2)]
    nslots = len(slots)
    per = blocks * 2
    factors, top = pl.pallas_call(
        functools.partial(upper_kernel, nslots, blocks),
        out_shape=(
            jax.ShapeDtypeStruct((3, E, count0 * 7 // 4), f32),
            jax.ShapeDtypeStruct((2, count0 // 4, F), f32),
        ),
        in_specs=smem(1) + vmem(nslots + 1),
        out_specs=tuple(vmem(2)),
        scratch_shapes=[
            pltpu.VMEM((nslots * blocks * 64, 128), f32),
            pltpu.VMEM((nslots * 8, 128), jnp.int32),
            pltpu.SMEM((nslots * 8, 128), jnp.int32),
            pltpu.SemaphoreType.DMA(()),
            pltpu.VMEM((4, 64, 2 * per * 128), f32),
            pltpu.VMEM((per * 64, 2 * per * 128), f32),
            pltpu.VMEM((per * 64, 256), bf16),
            pltpu.VMEM((E, 2 * EP), f32),
            pltpu.VMEM((2, E, EP), f32),
            pltpu.VMEM((2, EP, 3 * EP), f32),
            pltpu.VMEM((1, EP, 3 * EP), f32),
            pltpu.VMEM((2, E, EP), f32),
            pltpu.VMEM((2, 64, 128), f32),
            pltpu.VMEM((2, EP, 256), bf16),
            pltpu.VMEM((2, 256, 3 * EP), bf16),
            pltpu.VMEM((EP, 3 * EP), bf16),
            pltpu.VMEM((3 * EP, 2 * EP), bf16),
        ],
        compiler_params=pltpu.CompilerParams(vmem_limit_bytes=LIMIT),
    )(info, *slots, own0)
    return jnp.transpose(factors, (0, 2, 1))[:, None], top[:, None]


def solution(mesh):
    placed = (P("sub", "lm", None, None), P("sub", "lm"), P("sub", "lm"))
    return jax.shard_map(
        local,
        mesh=mesh,
        in_specs=placed,
        out_specs=(P(None, ("sub", "lm"), None, None), P(None, ("sub", "lm"), None, None)),
        check_vma=False,
    )
```

```python
import functools

import jax
import jax.numpy as jnp
from jax import lax
from jax.experimental import pallas as pl
from jax.experimental.pallas import tpu as pltpu
from jax.sharding import PartitionSpec as P

BW = 64
F = 1152
LEVELS = 3
E = 576
NB = E // BW
EP = 640
DAMPING = 1.0
f32 = jnp.float32
bf16 = jnp.bfloat16


def iota(shape, axis):
    return lax.broadcasted_iota(jnp.int32, shape, axis)


def row_of(x, t):
    return jnp.broadcast_to(x[t : t + 1, :], x.shape)


def col_of(x, j):
    return jnp.broadcast_to(x[:, j : j + 1], x.shape)


def split2(x):
    hi = x.astype(bf16)
    return hi, (x - hi.astype(f32)).astype(bf16)


def left3(dup):
    hi, lo = split2(dup)
    return jnp.concatenate([hi, lo[:, :64]], axis=1)


def right3(x):
    hi, lo = split2(x)
    return jnp.concatenate([hi, lo, hi], axis=0)


def dot(a, b):
    return jnp.dot(a, b, preferred_element_type=f32)


def dot_nt(a, b):
    return lax.dot_general(a, b, (((1,), (1,)), ((), ())), preferred_element_type=f32)


def roll64(x):
    return pltpu.roll(x, 64, 1)


def factor(mats):
    sub = iota((8, 128), 0)
    for kb in range(8):
        state = []
        for m in mats:
            x = m[kb]
            zero = x - x
            cols = [col_of(x, 8 * kb + t) + zero for t in range(8)]
            state.append([x, x, cols, jnp.ones((8, 128), f32), jnp.ones((8, 128), f32)])
        below = [
            [[col_of(m[v], 8 * kb + t) for t in range(8)] for v in range(kb + 1, 8)] for m in mats
        ]
        for t in range(8):
            for st in state:
                fwd, both, cols, diag, recip = st
                col = cols[t]
                d = row_of(col, t)
                rd = 1.0 / d
                st[3] = jnp.where(sub == t, d, diag)
                st[4] = jnp.where(sub == t, rd, recip)
                mult = jnp.where(sub == t, 0.0, col * rd)
                for t2 in range(t + 1, 8):
                    cols[t2] = cols[t2] - mult * row_of(cols[t2], t)
                st[1] = both - mult * row_of(both, t)
                st[0] = fwd - jnp.where(sub > t, mult, 0.0) * row_of(fwd, t)
        for b, m in enumerate(mats):
            fwd, both, cols, diag, recip = state[b]
            m[kb] = fwd * lax.rsqrt(diag)
            solved = both * recip
            rows = [row_of(solved, t) for t in range(8)]
            for v in range(kb + 1, 8):
                acc = None
                for t in range(8):
                    term = below[b][v - kb - 1][t] * rows[t]
                    acc = term if acc is None else acc + term
                m[v] = m[v] - acc
    return mats


def augmented(x):
    lane, row = iota((64, 128), 1), iota((64, 128), 0)
    full = jnp.where(lane < 64, x, jnp.where(lane - 64 == row, 1.0, 0.0))
    return [full[8 * v : 8 * v + 8] for v in range(8)]


def joined(rows):
    return jnp.concatenate(rows, axis=0)


def tiles_kernel(cam_ref, lm_ref, jac_ref, pay_ref, sum_ref):
    lane = iota((64, 128), 1)
    blocks = jac_ref.shape[0]
    sum_ref[...] = jnp.zeros_like(sum_ref)
    lane8, row8 = iota((8, 128), 1), iota((8, 128), 0)
    index = jnp.zeros((8, 128), f32)
    for n in range(blocks):
        j = jac_ref[n]
        t = lax.dot_general(j, j, (((0,), (0,)), ((), ())), preferred_element_type=f32)
        top, bottom = t[:64], t[64:]
        pay_ref[64 * n : 64 * n + 64, :] = jnp.where(lane < 64, roll64(top), bottom)
        c = cam_ref[n]
        cc = jnp.where(lane < 64, top, roll64(top))
        mine = (lane >= 64).astype(jnp.int32) == c % 2
        at = pl.ds(pl.multiple_of(c // 2 * 64, 64), 64)
        sum_ref[at, :] = sum_ref[at, :] + jnp.where(mine, cc, 0.0)
        index = jnp.where((lane8 == n) & (row8 == 0), c.astype(f32), index)
        index = jnp.where((lane8 == n) & (row8 == 1), lm_ref[n].astype(f32), index)
    pay_ref[64 * blocks :, :] = index


def bottom_kernel(info_ref, cam_ref, sum_a, sum_b, pay_ref, out_ref, own_ref, w_ref):
    lane, row = iota((64, 128), 1), iota((64, 128), 0)
    own_ref[...] = jnp.zeros_like(own_ref)
    mats = []
    for c in range(NB):
        at = slice(c // 2 * 64, c // 2 * 64 + 64)
        x = sum_a[at, :] + sum_b[at, :]
        if c % 2:
            x = roll64(x)
        mats.append(augmented(x + jnp.where(lane == row, 2 * DAMPING, 0.0)))
    mats = factor(mats)
    spread = info_ref[4]
    place = info_ref[1]
    count = own_ref.shape[1] // NB
    pick = (iota((128, count), 0) == iota((128, count), 1) * spread + place).astype(bf16)
    for c in range(NB):
        v = joined(mats[c])
        w = roll64(v)
        w_ref[c] = left3(jnp.where(lane < 64, w, v))
        upper = jnp.where((lane >= row) & (lane < 64), v, 0.0)
        hi, lo = split2(upper)
        own_ref[64 * c : 64 * c + 64, count * c : count * c + count] = dot(hi, pick) + dot(lo, pick)
    blocks = cam_ref.shape[0]
    for n in range(blocks):
        x = pay_ref[64 * n : 64 * n + 64, :]
        cl = jnp.where(lane < 64, x, roll64(x))
        y = dot(w_ref[cam_ref[n]], right3(cl))
        out_ref[64 * n : 64 * n + 64, :] = jnp.where(lane < 64, y, x)
    out_ref[64 * blocks :, :] = pay_ref[64 * blocks :, :]


def climb(a_ref, w_ref, l_ref, r_ref, batch):
    lane64 = iota((64, 128), 1)
    width = a_ref.shape[2]

    def inverse_of(mat):
        v = joined(mat)
        return left3(jnp.where(lane64 < 64, roll64(v), v))

    def finish(b, w, at, j):
        u = dot(w, right3(a_ref[b, at, :]))
        keep = iota((64, EP), 1) >= j * 64 + iota((64, EP), 0)
        us = jnp.where(keep, u[:, :EP], 0.0)
        a_ref[b, at, 0:EP] = us
        a_ref[b, at, EP:] = u[:, EP:]
        return us, u

    mats = factor([augmented(a_ref[b, 0:64, 0:128]) for b in range(batch)])
    for b in range(batch):
        w_ref[b] = inverse_of(mats[b])

    for first, last in ((1, 4), (4, 7), (7, 9)):
        low_row = 64 * first
        low_lane = low_row // 128 * 128
        starts = [low_lane] + list(range(EP, width, EP))
        sizes = [EP - low_lane] + [EP] * (len(starts) - 1)

        def step(j, carry, low_row=low_row, starts=starts, sizes=sizes):
            at = pl.ds(pl.multiple_of(j * 64 - 64, 64), 64)
            rows = pl.ds(pl.multiple_of(j * 64, 64), 64)
            wide = pl.ds(pl.multiple_of(j // 2 * 128, 128), 128)
            odd = j % 2 == 1
            olds = [w_ref[b] for b in range(batch)]
            mats = []
            for b in range(batch):
                us = dot(olds[b], right3(a_ref[b, at, wide]))
                swapped = roll64(us)
                us, other = jnp.where(odd, swapped, us), jnp.where(odd, us, swapped)
                dup = jnp.where(lane64 < 64, us, other)
                left = left3(-jnp.concatenate([dup, dup], axis=0).T[0:64])
                x = a_ref[b, rows, wide]
                x = jnp.where(odd, roll64(x), x)
                mats.append(augmented(x + dot(left, right3(us))))
            mats = factor(mats)
            for b in range(batch):
                us, u = finish(b, olds[b], at, j - 1)
                xs = jnp.where(iota((64, EP), 1) >= j * 64, -us, 0.0)
                l_ref[b] = left3(jnp.concatenate([xs, xs], axis=0).T)
                r_ref[b] = right3(u)
                left = l_ref[b, low_row:E]
                for s, size in zip(starts, sizes):
                    a_ref[b, low_row:E, s : s + size] = a_ref[b, low_row:E, s : s + size] + dot(
                        left, r_ref[b, :, s : s + size]
                    )
            for b in range(batch):
                w_ref[b] = inverse_of(mats[b])
            return carry

        lax.fori_loop(first, last, step, 0)
    for b in range(batch):
        finish(b, w_ref[b], slice(E - 64, E), NB - 1)


def gram_left(u, left_ref):
    hi, lo = split2((-u).T)
    left_ref[:, 0:EP] = hi
    left_ref[:, EP : 2 * EP] = hi
    left_ref[:, 2 * EP :] = lo


def spread_lanes(pick, u):
    hi, lo = split2(u)
    return dot(hi, pick) + dot(lo, pick)


def minus_rows(rows, u):
    count = rows.shape[0]
    hi, lo = split2(-rows)
    uh, ul = split2(u)
    both = dot(jnp.concatenate([hi, lo], axis=0), uh)
    return both[:count] + both[count:] + dot(hi, ul)


def upper_kernel(nslots, blocks, lm_count_static, info_ref, *refs):
    pays = refs[:nslots]
    own0_ref, fac_ref, top_ref = refs[nslots : nslots + 3]
    (all_ref, ivm, ism, sem, ydup, tbuf, lbuf, own_u0, odd_up, a1, a2, pri) = refs[nslots + 3 : nslots + 15]
    (w_ref, l_ref, r_ref, left_ref, right_ref) = refs[nslots + 15 :]
    lane = iota((64, 128), 1)
    me, my_lm = info_ref[0], info_ref[5]
    lm_count = lm_count_static
    per = blocks * nslots // 8

    for slot in range(nslots):
        s = me ^ (slot // 2)
        spot = s * 2 + (my_lm ^ (slot % 2))
        at = pl.ds(pl.multiple_of(spot * blocks * 64, 64), blocks * 64)
        all_ref[at, :] = pays[slot][0 : 64 * blocks, :]
        ivm[pl.ds(pl.multiple_of(spot * 8, 8), 8), :] = pays[slot][64 * blocks :, :].astype(jnp.int32)
    copy = pltpu.make_async_copy(ivm, ism, sem)
    copy.start()
    eye2 = jnp.where(iota((E, EP), 0) == iota((E, EP), 1), 2 * DAMPING, 0.0)
    own_u0[...] = jnp.zeros_like(own_u0)
    odd_up[...] = jnp.zeros_like(odd_up)
    for m in range(2):
        a1[m] = jnp.zeros(a1.shape[1:], f32)
        a1[m, 0:E, 0:EP] = eye2
        for v in range(EP // 128):
            pri[m * (EP // 128) + v] = 0.5 * eye2[:, 128 * v : 128 * v + 128]
    a2[0, 0:E, 0:EP] = eye2
    copy.wait()

    def ids(s, k):
        row = (s * 2 + k // blocks) * 8
        return ism[row, k % blocks], ism[row + 1, k % blocks]

    def rows64(i):
        return pl.ds(pl.multiple_of(i * 64, 64), 64)

    def lanes128(i):
        return pl.ds(pl.multiple_of(i * 128, 128), 128)

    def dups(s, k):
        x = all_ref[rows64(s * per + k), :]
        xr = roll64(x)
        return jnp.where(lane < 64, x, xr), jnp.where(lane < 64, xr, x)

    def half_of(l):
        return (lane >= 64).astype(jnp.int32) == l % 2

    for s in range(8):
        pair, half, merge = s // 2, s % 2, s // 4
        second = pair % 2

        def place(k, carry, s=s, pair=pair, half=half, merge=merge, second=second):
            c, l = ids(s, k)
            y, ll = dups(s, k)
            mine = half_of(l)
            ydup[pair, :, lanes128(half * per + k)] = y
            rows, lanes = rows64(l), lanes128(l // 2)
            ll = jnp.where(mine, ll, 0.0)
            if half == 0:
                a1[merge, rows, lanes] = a1[merge, rows, lanes] + ll
            elif second == 0:
                a2[0, rows, lanes] = a2[0, rows, lanes] + ll
            else:
                tile = merge * (EP // 128) + l // 2
                pri[tile, rows, :] = pri[tile, rows, :] + ll
                odd_up[merge, rows64(c), lanes] = odd_up[merge, rows64(c), lanes] + jnp.where(mine, y, 0.0)
            return carry

        lax.fori_loop(0, per, place, 0)

    my_pair = me // 2
    for half in range(2):

        def place_own(k, carry, half=half):
            c, l = ids(2 * my_pair + half, k)
            y, _ = dups(2 * my_pair + half, k)
            lanes = lanes128(half * (EP // 128) + l // 2)
            own_u0[rows64(c), lanes] = own_u0[rows64(c), lanes] + jnp.where(half_of(l), y, 0.0)
            return carry

        lax.fori_loop(0, per, place_own, 0)

    def gram_pair(p, carry):
        merge = p // 2

        def transposed(first):
            for k in range(per):
                t = ydup[p, :, 128 * (first + k) : 128 * (first + k + 1)]
                tt = jnp.concatenate([t, t], axis=0).T
                lbuf[64 * k : 64 * k + 64, :] = left3(-tt[0:64])

        def scatter(target, s_rows, halves, base):
            def body(n, carry):
                cn, ln = ids(s_rows, n)
                for i, h in enumerate(halves):
                    for k in range(per):
                        ck, lk = ids(2 * p + h, k)

                        @pl.when(ck == cn)
                        def _():
                            got = tbuf[rows64(n), 128 * (i * per + k) : 128 * (i * per + k + 1)]
                            to = pl.ds(pl.multiple_of(base[h] + lk // 2 * 128, 128), 128)
                            view = target.at[rows64(ln), to]
                            view[...] = view[...] + jnp.where(half_of(lk), got, 0.0)

                return carry

            lax.fori_loop(0, per, body, 0)

        transposed(0)
        wide = 128 * per
        for h in range(2):
            tbuf[:, h * wide : h * wide + wide] = dot(lbuf[...], right3(ydup[p, :, h * wide : h * wide + wide]))
        scatter(a1.at[merge], 2 * p, (0, 1), (0, EP + p % 2 * EP))

        @pl.when(p % 2 == 0)
        def _():
            transposed(per)
            tbuf[:, 0:wide] = dot(lbuf[...], right3(ydup[p, :, wide : 2 * wide]))
            scatter(a2.at[0], 2 * p + 1, (1,), (0, 0))

        return carry

    lax.fori_loop(0, 4, gram_pair, 0)

    climb(a1, w_ref, l_ref, r_ref, 2)

    def gram_merge(m, carry):
        u = a1[m, :, EP : 3 * EP]
        hi, lo = split2(u)
        right_ref[0:EP] = hi
        right_ref[EP : 2 * EP] = lo
        right_ref[2 * EP :] = hi
        gram_left(u[:, 0:EP], left_ref)
        a2[0, 0:E, 0:EP] = a2[0, 0:E, 0:EP] + dot(left_ref[0:E], right_ref[:, 0:EP])
        to = pl.ds(pl.multiple_of(EP + m * EP, 128), EP)
        a2[0, 0:E, to] = dot(left_ref[0:E], right_ref[:, EP : 2 * EP])
        return carry

    lax.fori_loop(0, 2, gram_merge, 0)

    climb(a2, w_ref, l_ref, r_ref, 1)

    def pick_of(count, spread, place):
        return (iota((EP, count), 0) == iota((EP, count), 1) * spread + place).astype(bf16)

    n0 = own0_ref.shape[1]
    n1, n2 = n0 // 2, n0 // 4
    merge = me // 4
    pick0 = pick_of(n0, 2 * lm_count, info_ref[1])
    pick1 = pick_of(n1, 4 * lm_count, info_ref[2])
    pick2 = pick_of(n2, 8 * lm_count, info_ref[3])
    fac_ref[0, :, 0:n0] = own0_ref[...]
    fac_ref[1, :, 0:n0] = spread_lanes(pick0, own_u0[:, 0:EP])
    fac_ref[2, :, 0:n0] = spread_lanes(pick0, own_u0[:, EP : 2 * EP])
    for t in range(3):
        fac_ref[t, :, n0 : n0 + n1] = spread_lanes(pick1, a1[merge, 0:E, t * EP : t * EP + EP])
    fac_ref[0, :, n0 + n1 : n0 + n1 + n2] = spread_lanes(pick2, a2[0, 0:E, 0:EP])

    def both_halves(low, up):
        r, c = iota((EP, 128), 0), iota((EP, 128), 1)
        source = c % 64 * (8 * lm_count) + info_ref[3]
        hit = (r == source) & (c % 64 < n2)
        at0 = (hit & (c < 64)).astype(bf16)
        at1 = (hit & (c >= 64)).astype(bf16)
        return spread_lanes(at0, low) + spread_lanes(at1, up)

    got = both_halves(a2[0, 0:E, EP : 2 * EP], a2[0, 0:E, 2 * EP : 3 * EP])
    fac_ref[1, :, n0 + n1 : n0 + n1 + n2] = got[:, 0:n2]
    fac_ref[2, :, n0 + n1 : n0 + n1 + n2] = got[:, 64 : 64 + n2]
    part = minus_rows(got.T, a2[0, 0:E, EP : 3 * EP])
    rows0 = both_halves(odd_up[0], odd_up[1]).T
    rows1 = both_halves(a1[0, 0:E, 2 * EP : 3 * EP], a1[1, 0:E, 2 * EP : 3 * EP]).T
    for h in range(2):
        own = minus_rows(rows0[64 * h : 64 * h + 64], odd_up[h])
        own = own + minus_rows(rows1[64 * h : 64 * h + 64], a1[h, 0:E, 2 * EP : 3 * EP])
        mine = pl.ds(info_ref[3], n2, stride=8 * lm_count)
        kept = [pri[h * (EP // 128) + v, mine, :] for v in range(EP // 128)]
        own = own[0:n2] + jnp.concatenate(kept, axis=1)
        for g in range(2):
            value = part[64 * h : 64 * h + n2, g * EP : g * EP + EP]
            if g == h:
                value = value + own
            top_ref[h, :, 0, g * E : g * E + E] = value[:, 0:E]


def vmem(n):
    return [pl.BlockSpec(memory_space=pltpu.VMEM)] * n


def smem(n):
    return [pl.BlockSpec(memory_space=pltpu.SMEM)] * n


LIMIT = 60 * 1024 * 1024


def local(jacobian, camera_block, landmark_block):
    lm_count = lax.axis_size("lm")
    sub_count = lax.axis_size("sub")
    lm_place = lax.axis_index("lm")
    sub_place = lax.axis_index("sub")
    group = 2**LEVELS
    jac = jacobian[0]
    blocks = jac.shape[0]

    def swap(value, sub_mask, lm_mask):
        pairs = [
            (s * lm_count + l, (s ^ sub_mask) * lm_count + (l ^ lm_mask))
            for s in range(sub_count)
            for l in range(lm_count)
        ]
        return lax.ppermute(value, ("sub", "lm"), pairs)

    info = jnp.stack(
        [
            sub_place % group,
            sub_place % 2 * lm_count + lm_place,
            sub_place % 4 * lm_count + lm_place,
            sub_place % 8 * lm_count + lm_place,
            jnp.int32(2 * lm_count),
            lm_place,
        ]
    ).astype(jnp.int32)
    cams = camera_block[0]
    lms = landmark_block[0] - NB
    payload = jax.ShapeDtypeStruct((64 * blocks + 8, 128), f32)

    pay, sums = pl.pallas_call(
        tiles_kernel,
        out_shape=(payload, jax.ShapeDtypeStruct(((NB + 1) // 2 * 64, 128), f32)),
        in_specs=smem(2) + vmem(1),
        out_specs=tuple(vmem(2)),
    )(cams, lms, jac)
    half_sums = sums + swap(sums, 1, 0)
    other_sums = swap(half_sums, 0, 1)

    count0 = E // (2 * lm_count)
    pay, own0 = pl.pallas_call(
        bottom_kernel,
        out_shape=(payload, jax.ShapeDtypeStruct((E, count0), f32)),
        in_specs=smem(2) + vmem(3),
        out_specs=tuple(vmem(2)),
        scratch_shapes=[pltpu.VMEM((NB, 64, 192), bf16)],
    )(info, cams, half_sums, other_sums, pay)

    held = {(0, 0): pay}
    for sub_mask, lm_mask in ((0, 1), (2, 0), (4, 0), (1, 0)):
        held.update({(q ^ sub_mask, l ^ lm_mask): swap(v, sub_mask, lm_mask) for (q, l), v in held.items()})
    slots = [held[q, l] for q in range(group) for l in range(2)]
    nslots = len(slots)
    per = blocks * 2
    factors, top = pl.pallas_call(
        functools.partial(upper_kernel, nslots, blocks, lm_count),
        out_shape=(
            jax.ShapeDtypeStruct((3, E, count0 * 7 // 4), f32),
            jax.ShapeDtypeStruct((2, count0 // 4, 1, F), f32),
        ),
        in_specs=smem(1) + vmem(nslots + 1),
        out_specs=tuple(vmem(2)),
        scratch_shapes=[
            pltpu.VMEM((nslots * blocks * 64, 128), f32),
            pltpu.VMEM((nslots * 8, 128), jnp.int32),
            pltpu.SMEM((nslots * 8, 128), jnp.int32),
            pltpu.SemaphoreType.DMA(()),
            pltpu.VMEM((4, 64, 2 * per * 128), f32),
            pltpu.VMEM((per * 64, 2 * per * 128), f32),
            pltpu.VMEM((per * 64, 192), bf16),
            pltpu.VMEM((E, 2 * EP), f32),
            pltpu.VMEM((2, E, EP), f32),
            pltpu.VMEM((2, EP, 3 * EP), f32),
            pltpu.VMEM((1, EP, 3 * EP), f32),
            pltpu.VMEM((2 * (EP // 128), E, 128), f32),
            pltpu.VMEM((2, 64, 192), bf16),
            pltpu.VMEM((2, EP, 192), bf16),
            pltpu.VMEM((2, 192, 3 * EP), bf16),
            pltpu.VMEM((EP, 3 * EP), bf16),
            pltpu.VMEM((3 * EP, 2 * EP), bf16),
        ],
        compiler_params=pltpu.CompilerParams(vmem_limit_bytes=LIMIT),
    )(info, *slots, own0)
    return jnp.transpose(factors, (0, 2, 1))[:, None], jnp.transpose(top, (0, 2, 1, 3))


def solution(mesh):
    placed = (P("sub", "lm", None, None), P("sub", "lm"), P("sub", "lm"))
    return jax.shard_map(
        local,
        mesh=mesh,
        in_specs=placed,
        out_specs=(P(None, ("sub", "lm"), None, None), P(None, ("sub", "lm"), None, None)),
        check_vma=False,
    )
```

```python
import functools

import jax
import jax.numpy as jnp
from jax import lax
from jax.experimental import pallas as pl
from jax.experimental.pallas import tpu as pltpu
from jax.sharding import PartitionSpec as P

BW = 64
F = 1152
LEVELS = 3
E = 576
NB = E // BW
EP = 640
DAMPING = 1.0
f32 = jnp.float32
bf16 = jnp.bfloat16


def iota(shape, axis):
    return lax.broadcasted_iota(jnp.int32, shape, axis)


def row_of(x, t):
    return jnp.broadcast_to(x[t : t + 1, :], x.shape)


def col_of(x, j):
    return jnp.broadcast_to(x[:, j : j + 1], x.shape)


def split2(x):
    hi = x.astype(bf16)
    return hi, (x - hi.astype(f32)).astype(bf16)


def left3(dup):
    hi, lo = split2(dup)
    return jnp.concatenate([hi, lo[:, :64]], axis=1)


def right3(x):
    hi, lo = split2(x)
    return jnp.concatenate([hi, lo, hi], axis=0)


def dot(a, b):
    return jnp.dot(a, b, preferred_element_type=f32)


def dot_nt(a, b):
    return lax.dot_general(a, b, (((1,), (1,)), ((), ())), preferred_element_type=f32)


def roll64(x):
    return pltpu.roll(x, 64, 1)


def factor(mats):
    sub = iota((8, 128), 0)
    zero = [m[0] - m[0] for m in mats]

    def spread(b, x, kb):
        return [col_of(x, 8 * kb + t) + zero[b] for t in range(8)]

    ready = [spread(b, m[0], 0) for b, m in enumerate(mats)]
    for kb in range(8):
        state, below = [], []
        for b, m in enumerate(mats):
            parts = [spread(b, m[v], kb) if v == kb + 1 else [col_of(m[v], 8 * kb + t) for t in range(8)] for v in range(kb + 1, 8)]
            below.append(parts)
            coming = spread(b, m[kb + 1], kb + 1) if kb < 7 else []
            ahead = list(parts[0]) if kb < 7 else []
            state.append([m[kb], m[kb], ready[b], jnp.ones((8, 128), f32), jnp.ones((8, 128), f32), ahead, coming])
        for t in range(8):
            for st in state:
                fwd, both, cols, diag, recip, ahead, coming = st
                col = cols[t]
                d = row_of(col, t)
                rd = 1.0 / d
                st[3] = jnp.where(sub == t, d, diag)
                st[4] = jnp.where(sub == t, rd, recip)
                mult = jnp.where(sub == t, 0.0, col * rd)
                for t2 in range(t + 1, 8):
                    cols[t2] = cols[t2] - mult * row_of(cols[t2], t)
                st[1] = both - mult * row_of(both, t)
                st[0] = fwd - jnp.where(sub > t, mult, 0.0) * row_of(fwd, t)
                if ahead:
                    weight = ahead[t]
                    scaled = weight * rd
                    for t2 in range(t + 1, 8):
                        ahead[t2] = ahead[t2] - scaled * row_of(col, t2)
                    for t2 in range(8):
                        coming[t2] = coming[t2] - weight * row_of(scaled, t2)
        for b, m in enumerate(mats):
            fwd, both, cols, diag, recip, ahead, coming = state[b]
            m[kb] = fwd * lax.rsqrt(diag)
            solved = both * recip
            rows = [row_of(solved, t) for t in range(8)]
            for v in range(kb + 1, 8):
                terms = [below[b][v - kb - 1][t] * rows[t] for t in range(8)]
                while len(terms) > 1:
                    terms = [x + y for x, y in zip(terms[0::2], terms[1::2])]
                m[v] = m[v] - terms[0]
            ready[b] = coming
    return mats


def augmented(x):
    lane, row = iota((64, 128), 1), iota((64, 128), 0)
    full = jnp.where(lane < 64, x, jnp.where(lane - 64 == row, 1.0, 0.0))
    return [full[8 * v : 8 * v + 8] for v in range(8)]


def joined(rows):
    return jnp.concatenate(rows, axis=0)


def tiles_kernel(cam_ref, lm_ref, jac_ref, pay_ref, sum_ref):
    lane = iota((64, 128), 1)
    blocks = jac_ref.shape[0]
    sum_ref[...] = jnp.zeros_like(sum_ref)
    lane8, row8 = iota((8, 128), 1), iota((8, 128), 0)
    index = jnp.zeros((8, 128), f32)
    for n in range(blocks):
        j = jac_ref[n]
        t = lax.dot_general(j, j, (((0,), (0,)), ((), ())), preferred_element_type=f32)
        top, bottom = t[:64], t[64:]
        pay_ref[64 * n : 64 * n + 64, :] = jnp.where(lane < 64, roll64(top), bottom)
        c = cam_ref[n]
        cc = jnp.where(lane < 64, top, roll64(top))
        mine = (lane >= 64).astype(jnp.int32) == c % 2
        at = pl.ds(pl.multiple_of(c // 2 * 64, 64), 64)
        sum_ref[at, :] = sum_ref[at, :] + jnp.where(mine, cc, 0.0)
        index = jnp.where((lane8 == n) & (row8 == 0), c.astype(f32), index)
        index = jnp.where((lane8 == n) & (row8 == 1), lm_ref[n].astype(f32), index)
    pay_ref[64 * blocks :, :] = index


def bottom_kernel(info_ref, cam_ref, sum_a, sum_b, pay_ref, out_ref, own_ref, w_ref):
    lane, row = iota((64, 128), 1), iota((64, 128), 0)
    own_ref[...] = jnp.zeros_like(own_ref)
    mats = []
    for c in range(NB):
        at = slice(c // 2 * 64, c // 2 * 64 + 64)
        x = sum_a[at, :] + sum_b[at, :]
        if c % 2:
            x = roll64(x)
        mats.append(augmented(x + jnp.where(lane == row, 2 * DAMPING, 0.0)))
    mats = factor(mats)
    spread = info_ref[4]
    place = info_ref[1]
    count = own_ref.shape[1] // NB
    pick = (iota((128, count), 0) == iota((128, count), 1) * spread + place).astype(bf16)
    for c in range(NB):
        v = joined(mats[c])
        w = roll64(v)
        w_ref[c] = left3(jnp.where(lane < 64, w, v))
        upper = jnp.where((lane >= row) & (lane < 64), v, 0.0)
        hi, lo = split2(upper)
        own_ref[64 * c : 64 * c + 64, count * c : count * c + count] = dot(hi, pick) + dot(lo, pick)
    blocks = cam_ref.shape[0]
    for n in range(blocks):
        x = pay_ref[64 * n : 64 * n + 64, :]
        cl = jnp.where(lane < 64, x, roll64(x))
        y = dot(w_ref[cam_ref[n]], right3(cl))
        out_ref[64 * n : 64 * n + 64, :] = jnp.where(lane < 64, y, x)
    out_ref[64 * blocks :, :] = pay_ref[64 * blocks :, :]


def climb(a_ref, w_ref, l_ref, r_ref, batch):
    lane64 = iota((64, 128), 1)
    width = a_ref.shape[2]

    def inverse_of(mat):
        v = joined(mat)
        return left3(jnp.where(lane64 < 64, roll64(v), v))

    def finish(b, w, at, j):
        u = dot(w, right3(a_ref[b, at, :]))
        keep = iota((64, EP), 1) >= j * 64 + iota((64, EP), 0)
        us = jnp.where(keep, u[:, :EP], 0.0)
        a_ref[b, at, 0:EP] = us
        a_ref[b, at, EP:] = u[:, EP:]
        return us, u

    mats = factor([augmented(a_ref[b, 0:64, 0:128]) for b in range(batch)])
    for b in range(batch):
        w_ref[b] = inverse_of(mats[b])

    for first, last in ((1, 4), (4, 7), (7, 9)):
        low_row = 64 * first
        low_lane = low_row // 128 * 128
        starts = [low_lane] + list(range(EP, width, EP))
        sizes = [EP - low_lane] + [EP] * (len(starts) - 1)

        def step(j, carry, low_row=low_row, starts=starts, sizes=sizes):
            at = pl.ds(pl.multiple_of(j * 64 - 64, 64), 64)
            rows = pl.ds(pl.multiple_of(j * 64, 64), 64)
            wide = pl.ds(pl.multiple_of(j // 2 * 128, 128), 128)
            odd = j % 2 == 1
            olds = [w_ref[b] for b in range(batch)]
            mats = []
            for b in range(batch):
                us = dot(olds[b], right3(a_ref[b, at, wide]))
                swapped = roll64(us)
                us, other = jnp.where(odd, swapped, us), jnp.where(odd, us, swapped)
                dup = jnp.where(lane64 < 64, us, other)
                left = left3(-jnp.concatenate([dup, dup], axis=0).T[0:64])
                x = a_ref[b, rows, wide]
                x = jnp.where(odd, roll64(x), x)
                mats.append(augmented(x + dot(left, right3(us))))
            mats = factor(mats)
            for b in range(batch):
                us, u = finish(b, olds[b], at, j - 1)
                xs = jnp.where(iota((64, EP), 1) >= j * 64, -us, 0.0)
                l_ref[b] = left3(jnp.concatenate([xs, xs], axis=0).T)
                r_ref[b] = right3(u)
                left = l_ref[b, low_row:E]
                for s, size in zip(starts, sizes):
                    a_ref[b, low_row:E, s : s + size] = a_ref[b, low_row:E, s : s + size] + dot(
                        left, r_ref[b, :, s : s + size]
                    )
            for b in range(batch):
                w_ref[b] = inverse_of(mats[b])
            return carry

        lax.fori_loop(first, last, step, 0)
    for b in range(batch):
        finish(b, w_ref[b], slice(E - 64, E), NB - 1)


def gram_left(u, left_ref):
    hi, lo = split2((-u).T)
    left_ref[:, 0:EP] = hi
    left_ref[:, EP : 2 * EP] = hi
    left_ref[:, 2 * EP :] = lo


def spread_lanes(pick, u):
    hi, lo = split2(u)
    return dot(hi, pick) + dot(lo, pick)


def minus_rows(rows, u):
    count = rows.shape[0]
    hi, lo = split2(-rows)
    uh, ul = split2(u)
    both = dot(jnp.concatenate([hi, lo], axis=0), uh)
    return both[:count] + both[count:] + dot(hi, ul)


def upper_kernel(nslots, blocks, lm_count_static, info_ref, *refs):
    pays = refs[:nslots]
    own0_ref, fac_ref, top_ref = refs[nslots : nslots + 3]
    (all_ref, ivm, ism, sem, ydup, tbuf, lbuf, own_u0, odd_up, a1, a2, pri) = refs[nslots + 3 : nslots + 15]
    (w_ref, l_ref, r_ref, left_ref, right_ref) = refs[nslots + 15 :]
    lane = iota((64, 128), 1)
    me, my_lm = info_ref[0], info_ref[5]
    lm_count = lm_count_static
    per = blocks * nslots // 8

    for slot in range(nslots):
        s = me ^ (slot // 2)
        spot = s * 2 + (my_lm ^ (slot % 2))
        at = pl.ds(pl.multiple_of(spot * blocks * 64, 64), blocks * 64)
        all_ref[at, :] = pays[slot][0 : 64 * blocks, :]
        ivm[pl.ds(pl.multiple_of(spot * 8, 8), 8), :] = pays[slot][64 * blocks :, :].astype(jnp.int32)
    copy = pltpu.make_async_copy(ivm, ism, sem)
    copy.start()
    eye2 = jnp.where(iota((E, EP), 0) == iota((E, EP), 1), 2 * DAMPING, 0.0)
    own_u0[...] = jnp.zeros_like(own_u0)
    odd_up[...] = jnp.zeros_like(odd_up)
    for m in range(2):
        a1[m] = jnp.zeros(a1.shape[1:], f32)
        a1[m, 0:E, 0:EP] = eye2
        for v in range(EP // 128):
            pri[m * (EP // 128) + v] = 0.5 * eye2[:, 128 * v : 128 * v + 128]
    a2[0, 0:E, 0:EP] = eye2
    copy.wait()

    def ids(s, k):
        row = (s * 2 + k // blocks) * 8
        return ism[row, k % blocks], ism[row + 1, k % blocks]

    def rows64(i):
        return pl.ds(pl.multiple_of(i * 64, 64), 64)

    def lanes128(i):
        return pl.ds(pl.multiple_of(i * 128, 128), 128)

    def dups(s, k):
        x = all_ref[rows64(s * per + k), :]
        xr = roll64(x)
        return jnp.where(lane < 64, x, xr), jnp.where(lane < 64, xr, x)

    def half_of(l):
        return (lane >= 64).astype(jnp.int32) == l % 2

    for s in range(8):
        pair, half, merge = s // 2, s % 2, s // 4
        second = pair % 2

        def place(k, carry, s=s, pair=pair, half=half, merge=merge, second=second):
            c, l = ids(s, k)
            y, ll = dups(s, k)
            mine = half_of(l)
            ydup[pair, :, lanes128(half * per + k)] = y
            rows, lanes = rows64(l), lanes128(l // 2)
            ll = jnp.where(mine, ll, 0.0)
            if half == 0:
                a1[merge, rows, lanes] = a1[merge, rows, lanes] + ll
            elif second == 0:
                a2[0, rows, lanes] = a2[0, rows, lanes] + ll
            else:
                tile = merge * (EP // 128) + l // 2
                pri[tile, rows, :] = pri[tile, rows, :] + ll
                odd_up[merge, rows64(c), lanes] = odd_up[merge, rows64(c), lanes] + jnp.where(mine, y, 0.0)
            return carry

        lax.fori_loop(0, per, place, 0)

    my_pair = me // 2
    for half in range(2):

        def place_own(k, carry, half=half):
            c, l = ids(2 * my_pair + half, k)
            y, _ = dups(2 * my_pair + half, k)
            lanes = lanes128(half * (EP // 128) + l // 2)
            own_u0[rows64(c), lanes] = own_u0[rows64(c), lanes] + jnp.where(half_of(l), y, 0.0)
            return carry

        lax.fori_loop(0, per, place_own, 0)

    def gram_pair(p, carry):
        merge = p // 2

        def transposed(first):
            for k in range(per):
                t = ydup[p, :, 128 * (first + k) : 128 * (first + k + 1)]
                tt = jnp.concatenate([t, t], axis=0).T
                lbuf[64 * k : 64 * k + 64, :] = left3(-tt[0:64])

        def scatter(target, s_rows, halves, base):
            def body(n, carry):
                cn, ln = ids(s_rows, n)
                for i, h in enumerate(halves):
                    for k in range(per):
                        ck, lk = ids(2 * p + h, k)

                        @pl.when(ck == cn)
                        def _():
                            got = tbuf[rows64(n), 128 * (i * per + k) : 128 * (i * per + k + 1)]
                            to = pl.ds(pl.multiple_of(base[h] + lk // 2 * 128, 128), 128)
                            view = target.at[rows64(ln), to]
                            view[...] = view[...] + jnp.where(half_of(lk), got, 0.0)

                return carry

            lax.fori_loop(0, per, body, 0)

        transposed(0)
        wide = 128 * per
        for h in range(2):
            tbuf[:, h * wide : h * wide + wide] = dot(lbuf[...], right3(ydup[p, :, h * wide : h * wide + wide]))
        scatter(a1.at[merge], 2 * p, (0, 1), (0, EP + p % 2 * EP))

        @pl.when(p % 2 == 0)
        def _():
            transposed(per)
            tbuf[:, 0:wide] = dot(lbuf[...], right3(ydup[p, :, wide : 2 * wide]))
            scatter(a2.at[0], 2 * p + 1, (1,), (0, 0))

        return carry

    lax.fori_loop(0, 4, gram_pair, 0)

    climb(a1, w_ref, l_ref, r_ref, 2)

    def gram_merge(m, carry):
        u = a1[m, :, EP : 3 * EP]
        hi, lo = split2(u)
        right_ref[0:EP] = hi
        right_ref[EP : 2 * EP] = lo
        right_ref[2 * EP :] = hi
        gram_left(u[:, 0:EP], left_ref)
        a2[0, 0:E, 0:EP] = a2[0, 0:E, 0:EP] + dot(left_ref[0:E], right_ref[:, 0:EP])
        to = pl.ds(pl.multiple_of(EP + m * EP, 128), EP)
        a2[0, 0:E, to] = dot(left_ref[0:E], right_ref[:, EP : 2 * EP])
        return carry

    lax.fori_loop(0, 2, gram_merge, 0)

    climb(a2, w_ref, l_ref, r_ref, 1)

    def pick_of(count, spread, place):
        return (iota((EP, count), 0) == iota((EP, count), 1) * spread + place).astype(bf16)

    n0 = own0_ref.shape[1]
    n1, n2 = n0 // 2, n0 // 4
    merge = me // 4
    pick0 = pick_of(n0, 2 * lm_count, info_ref[1])
    pick1 = pick_of(n1, 4 * lm_count, info_ref[2])
    pick2 = pick_of(n2, 8 * lm_count, info_ref[3])
    fac_ref[0, :, 0:n0] = own0_ref[...]
    fac_ref[1, :, 0:n0] = spread_lanes(pick0, own_u0[:, 0:EP])
    fac_ref[2, :, 0:n0] = spread_lanes(pick0, own_u0[:, EP : 2 * EP])
    for t in range(3):
        fac_ref[t, :, n0 : n0 + n1] = spread_lanes(pick1, a1[merge, 0:E, t * EP : t * EP + EP])
    fac_ref[0, :, n0 + n1 : n0 + n1 + n2] = spread_lanes(pick2, a2[0, 0:E, 0:EP])

    def both_halves(low, up):
        r, c = iota((EP, 128), 0), iota((EP, 128), 1)
        source = c % 64 * (8 * lm_count) + info_ref[3]
        hit = (r == source) & (c % 64 < n2)
        at0 = (hit & (c < 64)).astype(bf16)
        at1 = (hit & (c >= 64)).astype(bf16)
        return spread_lanes(at0, low) + spread_lanes(at1, up)

    got = both_halves(a2[0, 0:E, EP : 2 * EP], a2[0, 0:E, 2 * EP : 3 * EP])
    fac_ref[1, :, n0 + n1 : n0 + n1 + n2] = got[:, 0:n2]
    fac_ref[2, :, n0 + n1 : n0 + n1 + n2] = got[:, 64 : 64 + n2]
    part = minus_rows(got.T, a2[0, 0:E, EP : 3 * EP])
    rows0 = both_halves(odd_up[0], odd_up[1]).T
    rows1 = both_halves(a1[0, 0:E, 2 * EP : 3 * EP], a1[1, 0:E, 2 * EP : 3 * EP]).T
    for h in range(2):
        own = minus_rows(rows0[64 * h : 64 * h + 64], odd_up[h])
        own = own + minus_rows(rows1[64 * h : 64 * h + 64], a1[h, 0:E, 2 * EP : 3 * EP])
        mine = pl.ds(info_ref[3], n2, stride=8 * lm_count)
        kept = [pri[h * (EP // 128) + v, mine, :] for v in range(EP // 128)]
        own = own[0:n2] + jnp.concatenate(kept, axis=1)
        for g in range(2):
            value = part[64 * h : 64 * h + n2, g * EP : g * EP + EP]
            if g == h:
                value = value + own
            top_ref[h, :, 0, g * E : g * E + E] = value[:, 0:E]


def vmem(n):
    return [pl.BlockSpec(memory_space=pltpu.VMEM)] * n


def smem(n):
    return [pl.BlockSpec(memory_space=pltpu.SMEM)] * n


LIMIT = 60 * 1024 * 1024


def local(jacobian, camera_block, landmark_block):
    lm_count = lax.axis_size("lm")
    sub_count = lax.axis_size("sub")
    lm_place = lax.axis_index("lm")
    sub_place = lax.axis_index("sub")
    group = 2**LEVELS
    jac = jacobian[0]
    blocks = jac.shape[0]

    def swap(value, sub_mask, lm_mask):
        pairs = [
            (s * lm_count + l, (s ^ sub_mask) * lm_count + (l ^ lm_mask))
            for s in range(sub_count)
            for l in range(lm_count)
        ]
        return lax.ppermute(value, ("sub", "lm"), pairs)

    info = jnp.stack(
        [
            sub_place % group,
            sub_place % 2 * lm_count + lm_place,
            sub_place % 4 * lm_count + lm_place,
            sub_place % 8 * lm_count + lm_place,
            jnp.int32(2 * lm_count),
            lm_place,
        ]
    ).astype(jnp.int32)
    cams = camera_block[0]
    lms = landmark_block[0] - NB
    payload = jax.ShapeDtypeStruct((64 * blocks + 8, 128), f32)

    pay, sums = pl.pallas_call(
        tiles_kernel,
        out_shape=(payload, jax.ShapeDtypeStruct(((NB + 1) // 2 * 64, 128), f32)),
        in_specs=smem(2) + vmem(1),
        out_specs=tuple(vmem(2)),
    )(cams, lms, jac)
    half_sums = sums + swap(sums, 1, 0)
    other_sums = swap(half_sums, 0, 1)

    count0 = E // (2 * lm_count)
    pay, own0 = pl.pallas_call(
        bottom_kernel,
        out_shape=(payload, jax.ShapeDtypeStruct((E, count0), f32)),
        in_specs=smem(2) + vmem(3),
        out_specs=tuple(vmem(2)),
        scratch_shapes=[pltpu.VMEM((NB, 64, 192), bf16)],
    )(info, cams, half_sums, other_sums, pay)

    held = {(0, 0): pay}
    for sub_mask, lm_mask in ((0, 1), (2, 0), (4, 0), (1, 0)):
        held.update({(q ^ sub_mask, l ^ lm_mask): swap(v, sub_mask, lm_mask) for (q, l), v in held.items()})
    slots = [held[q, l] for q in range(group) for l in range(2)]
    nslots = len(slots)
    per = blocks * 2
    factors, top = pl.pallas_call(
        functools.partial(upper_kernel, nslots, blocks, lm_count),
        out_shape=(
            jax.ShapeDtypeStruct((3, E, count0 * 7 // 4), f32),
            jax.ShapeDtypeStruct((2, count0 // 4, 1, F), f32),
        ),
        in_specs=smem(1) + vmem(nslots + 1),
        out_specs=tuple(vmem(2)),
        scratch_shapes=[
            pltpu.VMEM((nslots * blocks * 64, 128), f32),
            pltpu.VMEM((nslots * 8, 128), jnp.int32),
            pltpu.SMEM((nslots * 8, 128), jnp.int32),
            pltpu.SemaphoreType.DMA(()),
            pltpu.VMEM((4, 64, 2 * per * 128), f32),
            pltpu.VMEM((per * 64, 2 * per * 128), f32),
            pltpu.VMEM((per * 64, 192), bf16),
            pltpu.VMEM((E, 2 * EP), f32),
            pltpu.VMEM((2, E, EP), f32),
            pltpu.VMEM((2, EP, 3 * EP), f32),
            pltpu.VMEM((1, EP, 3 * EP), f32),
            pltpu.VMEM((2 * (EP // 128), E, 128), f32),
            pltpu.VMEM((2, 64, 192), bf16),
            pltpu.VMEM((2, EP, 192), bf16),
            pltpu.VMEM((2, 192, 3 * EP), bf16),
            pltpu.VMEM((EP, 3 * EP), bf16),
            pltpu.VMEM((3 * EP, 2 * EP), bf16),
        ],
        compiler_params=pltpu.CompilerParams(vmem_limit_bytes=LIMIT),
    )(info, *slots, own0)
    return jnp.transpose(factors, (0, 2, 1))[:, None], jnp.transpose(top, (0, 2, 1, 3))


def solution(mesh):
    placed = (P("sub", "lm", None, None), P("sub", "lm"), P("sub", "lm"))
    return jax.shard_map(
        local,
        mesh=mesh,
        in_specs=placed,
        out_specs=(P(None, ("sub", "lm"), None, None), P(None, ("sub", "lm"), None, None)),
        check_vma=False,
    )
```

```python
import functools

import jax
import jax.numpy as jnp
from jax import lax
from jax.experimental import pallas as pl
from jax.experimental.pallas import tpu as pltpu
from jax.sharding import PartitionSpec as P

BW = 64
F = 1152
LEVELS = 3
E = 576
NB = E // BW
EP = 640
DAMPING = 1.0
f32 = jnp.float32
bf16 = jnp.bfloat16


def iota(shape, axis):
    return lax.broadcasted_iota(jnp.int32, shape, axis)


def row_of(x, t):
    return jnp.broadcast_to(x[t : t + 1, :], x.shape)


def col_of(x, j):
    return jnp.broadcast_to(x[:, j : j + 1], x.shape)


def split2(x):
    hi = x.astype(bf16)
    return hi, (x - hi.astype(f32)).astype(bf16)


def left3(dup):
    hi, lo = split2(dup)
    return jnp.concatenate([hi, lo[:, :64]], axis=1)


def right3(x):
    hi, lo = split2(x)
    return jnp.concatenate([hi, lo, hi], axis=0)


def dot(a, b):
    return jnp.dot(a, b, preferred_element_type=f32)


def dot_nt(a, b):
    return lax.dot_general(a, b, (((1,), (1,)), ((), ())), preferred_element_type=f32)


def roll64(x):
    return pltpu.roll(x, 64, 1)


def factor(mats):
    sub = iota((8, 128), 0)
    zero = [m[0] - m[0] for m in mats]

    def spread(b, x, kb):
        return [col_of(x, 8 * kb + t) + zero[b] for t in range(8)]

    ready = [spread(b, m[0], 0) for b, m in enumerate(mats)]
    for kb in range(8):
        state, below = [], []
        for b, m in enumerate(mats):
            parts = [spread(b, m[v], kb) if v == kb + 1 else [col_of(m[v], 8 * kb + t) for t in range(8)] for v in range(kb + 1, 8)]
            below.append(parts)
            coming = spread(b, m[kb + 1], kb + 1) if kb < 7 else []
            ahead = list(parts[0]) if kb < 7 else []
            state.append([m[kb], m[kb], ready[b], jnp.ones((8, 128), f32), jnp.ones((8, 128), f32), ahead, coming])
        for t in range(8):
            for st in state:
                fwd, both, cols, diag, recip, ahead, coming = st
                col = cols[t]
                d = row_of(col, t)
                rd = 1.0 / d
                st[3] = jnp.where(sub == t, d, diag)
                st[4] = jnp.where(sub == t, rd, recip)
                mult = jnp.where(sub == t, 0.0, col * rd)
                for t2 in range(t + 1, 8):
                    cols[t2] = cols[t2] - mult * row_of(cols[t2], t)
                st[1] = both - mult * row_of(both, t)
                st[0] = fwd - jnp.where(sub > t, mult, 0.0) * row_of(fwd, t)
                if ahead:
                    weight = ahead[t]
                    scaled = weight * rd
                    for t2 in range(t + 1, 8):
                        ahead[t2] = ahead[t2] - scaled * row_of(col, t2)
                    for t2 in range(8):
                        coming[t2] = coming[t2] - weight * row_of(scaled, t2)
        for b, m in enumerate(mats):
            fwd, both, cols, diag, recip, ahead, coming = state[b]
            m[kb] = fwd * lax.rsqrt(diag)
            solved = both * recip
            rows = [row_of(solved, t) for t in range(8)]
            for v in range(kb + 1, 8):
                terms = [below[b][v - kb - 1][t] * rows[t] for t in range(8)]
                while len(terms) > 1:
                    terms = [x + y for x, y in zip(terms[0::2], terms[1::2])]
                m[v] = m[v] - terms[0]
            ready[b] = coming
    return mats


def augmented(x):
    lane, row = iota((64, 128), 1), iota((64, 128), 0)
    full = jnp.where(lane < 64, x, jnp.where(lane - 64 == row, 1.0, 0.0))
    return [full[8 * v : 8 * v + 8] for v in range(8)]


def joined(rows):
    return jnp.concatenate(rows, axis=0)


def tiles_kernel(cam_ref, lm_ref, jac_ref, pay_ref, sum_ref):
    lane = iota((64, 128), 1)
    blocks = jac_ref.shape[0]
    sum_ref[...] = jnp.zeros_like(sum_ref)
    lane8, row8 = iota((8, 128), 1), iota((8, 128), 0)
    row, col = iota((64, 128), 0), lane % 64
    index = jnp.zeros((8, 128), f32)
    tops, lls = [], []
    for n in range(blocks):
        j = jac_ref[n]
        t = lax.dot_general(j, j, (((0,), (0,)), ((), ())), preferred_element_type=f32)
        top = t[:64]
        tops.append(top)
        lls.append(t[64:])
        c = cam_ref[n]
        cc = jnp.where(lane < 64, top, roll64(top))
        mine = (lane >= 64).astype(jnp.int32) == c % 2
        at = pl.ds(pl.multiple_of(c // 2 * 64, 64), 64)
        sum_ref[at, :] = sum_ref[at, :] + jnp.where(mine, cc, 0.0)
        index = jnp.where((lane8 == n) & (row8 == 0), c.astype(f32), index)
        index = jnp.where((lane8 == n) & (row8 == 1), lm_ref[n].astype(f32), index)
    for k in range(blocks // 2):
        both = jnp.where(lane < 64, roll64(tops[2 * k]), tops[2 * k + 1])
        pay_ref[64 * k : 64 * k + 64, :] = both
    for k in range(blocks // 4):
        first = jnp.where(lane < 64, roll64(lls[4 * k]), lls[4 * k + 2])
        second = jnp.where(lane < 64, roll64(lls[4 * k + 1]), lls[4 * k + 3])
        base = 64 * (blocks // 2 + k)
        pay_ref[base : base + 64, :] = jnp.where(row >= col, first, second)
        diag = jnp.sum(jnp.where(row == col, second, 0.0), axis=0, keepdims=True)
        index = jnp.where(row8 == 2 + k, jnp.broadcast_to(diag, (8, 128)), index)
    pay_ref[64 * (3 * blocks // 4) :, :] = index


def bottom_kernel(info_ref, cam_ref, sum_a, sum_b, pay_ref, out_ref, own_ref, w_ref, v_ref):
    lane, row = iota((64, 128), 1), iota((64, 128), 0)
    own_ref[...] = jnp.zeros_like(own_ref)
    together = 3

    def several(g, carry):
        mats = []
        for i in range(together):
            c = g * together + i
            at = pl.ds(pl.multiple_of(c // 2 * 64, 64), 64)
            x = sum_a[at, :] + sum_b[at, :]
            x = jnp.where(c % 2 == 1, roll64(x), x)
            mats.append(augmented(x + jnp.where(lane == row, 2 * DAMPING, 0.0)))
        mats = factor(mats)
        for i in range(together):
            v_ref[g * together + i] = joined(mats[i])
        return carry

    lax.fori_loop(0, NB // together, several, 0)
    spread = info_ref[4]
    place = info_ref[1]
    count = own_ref.shape[1] // NB
    pick = (iota((128, count), 0) == iota((128, count), 1) * spread + place).astype(bf16)
    for c in range(NB):
        v = v_ref[c]
        w = roll64(v)
        w_ref[c] = left3(jnp.where(lane < 64, w, v))
        upper = jnp.where((lane >= row) & (lane < 64), v, 0.0)
        hi, lo = split2(upper)
        own_ref[64 * c : 64 * c + 64, count * c : count * c + count] = dot(hi, pick) + dot(lo, pick)
    blocks = cam_ref.shape[0]
    for k in range(blocks // 2):
        x = pay_ref[64 * k : 64 * k + 64, :]
        xr = roll64(x)
        y0 = dot(w_ref[cam_ref[2 * k]], right3(jnp.where(lane < 64, x, xr)))
        y1 = dot(w_ref[cam_ref[2 * k + 1]], right3(jnp.where(lane < 64, xr, x)))
        out_ref[64 * k : 64 * k + 64, :] = jnp.where(lane < 64, y0, y1)
    out_ref[32 * blocks :, :] = pay_ref[32 * blocks :, :]


def climb(a_ref, w_ref, n_ref, l_ref, r_ref, batch):
    lane64 = iota((64, 128), 1)
    width = a_ref.shape[2]

    def keep_inverse(b, mat):
        v = joined(mat)
        hi, lo = split2(jnp.where(lane64 < 64, roll64(v), v))
        w_ref[b] = jnp.concatenate([hi, lo[:, :64]], axis=1)
        n = jnp.concatenate([jnp.where(lane64 < 64, hi, lo), hi[:, :64]], axis=1)
        n_ref[b] = jnp.concatenate([n, n], axis=0)

    def finish(b, w, at, j):
        u = dot(w, right3(a_ref[b, at, :]))
        keep = iota((64, EP), 1) >= j * 64 + iota((64, EP), 0)
        us = jnp.where(keep, u[:, :EP], 0.0)
        a_ref[b, at, 0:EP] = us
        a_ref[b, at, EP:] = u[:, EP:]
        return us, u

    mats = factor([augmented(a_ref[b, 0:64, 0:128]) for b in range(batch)])
    for b in range(batch):
        keep_inverse(b, mats[b])

    for first, last in ((1, 4), (4, 7), (7, 9)):
        low_row = 64 * first
        low_lane = low_row // 128 * 128
        starts = [low_lane] + list(range(EP, width, EP))
        sizes = [EP - low_lane] + [EP] * (len(starts) - 1)

        def step(j, carry, low_row=low_row, starts=starts, sizes=sizes):
            at = pl.ds(pl.multiple_of(j * 64 - 64, 64), 64)
            rows = pl.ds(pl.multiple_of(j * 64, 64), 64)
            wide = pl.ds(pl.multiple_of(j // 2 * 128, 128), 128)
            narrow = pl.ds(pl.multiple_of((j - 1) // 2 * 128, 128), 128)
            odd = j % 2 == 1
            olds = [w_ref[b] for b in range(batch)]
            mats = []
            for b in range(batch):
                us = dot(olds[b], right3(a_ref[b, at, wide]))
                us = jnp.where(odd, roll64(us), us)
                side = a_ref[b, rows, narrow]
                turned = roll64(side)
                side = jnp.where((lane64 < 64) == odd, side, turned)
                left = left3(-dot_nt(left3(side), n_ref[b]))
                x = a_ref[b, rows, wide]
                x = jnp.where(odd, roll64(x), x)
                mats.append(augmented(x + dot(left, right3(us))))
            mats = factor(mats)
            for b in range(batch):
                us, u = finish(b, olds[b], at, j - 1)
                xs = jnp.where(iota((64, EP), 1) >= j * 64, -us, 0.0)
                l_ref[b] = left3(jnp.concatenate([xs, xs], axis=0).T)
                r_ref[b] = right3(u)
                left = l_ref[b, low_row:E]
                for s, size in zip(starts, sizes):
                    a_ref[b, low_row:E, s : s + size] = a_ref[b, low_row:E, s : s + size] + dot(
                        left, r_ref[b, :, s : s + size]
                    )
            for b in range(batch):
                keep_inverse(b, mats[b])
            return carry

        lax.fori_loop(first, last, step, 0)
    for b in range(batch):
        finish(b, w_ref[b], slice(E - 64, E), NB - 1)


def gram_left(u, left_ref):
    hi, lo = split2((-u).T)
    left_ref[:, 0:EP] = hi
    left_ref[:, EP : 2 * EP] = hi
    left_ref[:, 2 * EP :] = lo


def spread_lanes(pick, u):
    hi, lo = split2(u)
    return dot(hi, pick) + dot(lo, pick)


def minus_rows(rows, u):
    count = rows.shape[0]
    hi, lo = split2(-rows)
    uh, ul = split2(u)
    both = dot(jnp.concatenate([hi, lo], axis=0), uh)
    return both[:count] + both[count:] + dot(hi, ul)


def upper_kernel(nslots, blocks, lm_count_static, info_ref, *refs):
    pays = refs[:nslots]
    own0_ref, fac_ref, top_ref = refs[nslots : nslots + 3]
    (all_ref, ivm, ism, sem, ydup, tbuf, lbuf, own_u0, odd_up, a1, a2, pri) = refs[nslots + 3 : nslots + 15]
    (w_ref, n_ref, l_ref, r_ref, left_ref, right_ref) = refs[nslots + 15 :]
    lane, row = iota((64, 128), 1), iota((64, 128), 0)
    col = lane % 64
    me, my_lm = info_ref[0], info_ref[5]
    lm_count = lm_count_static
    per = blocks * nslots // 8

    for slot in range(nslots):
        s = me ^ (slot // 2)
        spot = s * 2 + (my_lm ^ (slot % 2))
        tail = pays[slot][48 * blocks : 48 * blocks + 8, :]
        ivm[pl.ds(pl.multiple_of(spot * 8, 8), 8), :] = tail.astype(jnp.int32)
        for k in range(blocks // 4):
            base = 64 * (blocks // 2 + k)
            packed = pays[slot][base : base + 64, :]
            turned = jnp.concatenate([packed, packed], axis=0).T
            turned = jnp.where(lane < 64, turned[0:64], turned[64:128])
            diag = jnp.broadcast_to(tail[2 + k : 3 + k, :], (64, 128))
            first = jnp.where(row >= col, packed, turned)
            second = jnp.where(row < col, packed, jnp.where(row > col, turned, diag))
            for i in range(2):
                y = pays[slot][64 * (2 * k + i) : 64 * (2 * k + i) + 64, :]
                yr = roll64(y)
                for h, ll in enumerate((first, second)):
                    at = pl.ds(pl.multiple_of((spot * blocks + 4 * k + 2 * i + h) * 64, 64), 64)
                    ll = ll if i else roll64(ll)
                    all_ref[at, :] = jnp.where(lane < 64, yr if h else y, ll)
    copy = pltpu.make_async_copy(ivm, ism, sem)
    copy.start()
    eye2 = jnp.where(iota((E, EP), 0) == iota((E, EP), 1), 2 * DAMPING, 0.0)
    own_u0[...] = jnp.zeros_like(own_u0)
    odd_up[...] = jnp.zeros_like(odd_up)
    for m in range(2):
        a1[m] = jnp.zeros(a1.shape[1:], f32)
        a1[m, 0:E, 0:EP] = eye2
        for v in range(EP // 128):
            pri[m * (EP // 128) + v] = 0.5 * eye2[:, 128 * v : 128 * v + 128]
    a2[0, 0:E, 0:EP] = eye2
    copy.wait()

    def ids(s, k):
        row = (s * 2 + k // blocks) * 8
        return ism[row, k % blocks], ism[row + 1, k % blocks]

    def rows64(i):
        return pl.ds(pl.multiple_of(i * 64, 64), 64)

    def lanes128(i):
        return pl.ds(pl.multiple_of(i * 128, 128), 128)

    def dups(s, k):
        x = all_ref[rows64(s * per + k), :]
        xr = roll64(x)
        return jnp.where(lane < 64, x, xr), jnp.where(lane < 64, xr, x)

    def half_of(l):
        return (lane >= 64).astype(jnp.int32) == l % 2

    for s in range(8):
        pair, half, merge = s // 2, s % 2, s // 4
        second = pair % 2

        def place(k, carry, s=s, pair=pair, half=half, merge=merge, second=second):
            c, l = ids(s, k)
            y, ll = dups(s, k)
            mine = half_of(l)
            ydup[pair, :, lanes128(half * per + k)] = y
            rows, lanes = rows64(l), lanes128(l // 2)
            ll = jnp.where(mine, ll, 0.0)
            if half == 0:
                a1[merge, rows, lanes] = a1[merge, rows, lanes] + ll
            elif second == 0:
                a2[0, rows, lanes] = a2[0, rows, lanes] + ll
            else:
                tile = merge * (EP // 128) + l // 2
                pri[tile, rows, :] = pri[tile, rows, :] + ll
                odd_up[merge, rows64(c), lanes] = odd_up[merge, rows64(c), lanes] + jnp.where(mine, y, 0.0)
            return carry

        lax.fori_loop(0, per, place, 0)

    my_pair = me // 2
    for half in range(2):

        def place_own(k, carry, half=half):
            c, l = ids(2 * my_pair + half, k)
            y, _ = dups(2 * my_pair + half, k)
            lanes = lanes128(half * (EP // 128) + l // 2)
            own_u0[rows64(c), lanes] = own_u0[rows64(c), lanes] + jnp.where(half_of(l), y, 0.0)
            return carry

        lax.fori_loop(0, per, place_own, 0)

    def gram_pair(p, carry):
        merge = p // 2

        def transposed(first):
            for k in range(per):
                t = ydup[p, :, 128 * (first + k) : 128 * (first + k + 1)]
                tt = jnp.concatenate([t, t], axis=0).T
                lbuf[64 * k : 64 * k + 64, :] = left3(-tt[0:64])

        def scatter(target, s_rows, halves, base):
            def body(n, carry):
                cn, ln = ids(s_rows, n)
                for i, h in enumerate(halves):
                    for k in range(per):
                        ck, lk = ids(2 * p + h, k)

                        @pl.when(ck == cn)
                        def _():
                            got = tbuf[rows64(n), 128 * (i * per + k) : 128 * (i * per + k + 1)]
                            to = pl.ds(pl.multiple_of(base[h] + lk // 2 * 128, 128), 128)
                            view = target.at[rows64(ln), to]
                            view[...] = view[...] + jnp.where(half_of(lk), got, 0.0)

                return carry

            lax.fori_loop(0, per, body, 0)

        transposed(0)
        wide = 128 * per
        for h in range(2):
            tbuf[:, h * wide : h * wide + wide] = dot(lbuf[...], right3(ydup[p, :, h * wide : h * wide + wide]))
        scatter(a1.at[merge], 2 * p, (0, 1), (0, EP + p % 2 * EP))

        @pl.when(p % 2 == 0)
        def _():
            transposed(per)
            tbuf[:, 0:wide] = dot(lbuf[...], right3(ydup[p, :, wide : 2 * wide]))
            scatter(a2.at[0], 2 * p + 1, (1,), (0, 0))

        return carry

    lax.fori_loop(0, 4, gram_pair, 0)

    climb(a1, w_ref, n_ref, l_ref, r_ref, 2)

    def gram_merge(m, carry):
        u = a1[m, :, EP : 3 * EP]
        hi, lo = split2(u)
        right_ref[0:EP] = hi
        right_ref[EP : 2 * EP] = lo
        right_ref[2 * EP :] = hi
        gram_left(u[:, 0:EP], left_ref)
        a2[0, 0:E, 0:EP] = a2[0, 0:E, 0:EP] + dot(left_ref[0:E], right_ref[:, 0:EP])
        to = pl.ds(pl.multiple_of(EP + m * EP, 128), EP)
        a2[0, 0:E, to] = dot(left_ref[0:E], right_ref[:, EP : 2 * EP])
        return carry

    lax.fori_loop(0, 2, gram_merge, 0)

    climb(a2, w_ref, n_ref, l_ref, r_ref, 1)

    def pick_of(count, spread, place):
        return (iota((EP, count), 0) == iota((EP, count), 1) * spread + place).astype(bf16)

    n0 = own0_ref.shape[1]
    n1, n2 = n0 // 2, n0 // 4
    merge = me // 4
    pick0 = pick_of(n0, 2 * lm_count, info_ref[1])
    pick1 = pick_of(n1, 4 * lm_count, info_ref[2])
    pick2 = pick_of(n2, 8 * lm_count, info_ref[3])
    fac_ref[0, :, 0:n0] = own0_ref[...]
    fac_ref[1, :, 0:n0] = spread_lanes(pick0, own_u0[:, 0:EP])
    fac_ref[2, :, 0:n0] = spread_lanes(pick0, own_u0[:, EP : 2 * EP])
    for t in range(3):
        fac_ref[t, :, n0 : n0 + n1] = spread_lanes(pick1, a1[merge, 0:E, t * EP : t * EP + EP])
    fac_ref[0, :, n0 + n1 : n0 + n1 + n2] = spread_lanes(pick2, a2[0, 0:E, 0:EP])

    def both_halves(low, up):
        r, c = iota((EP, 128), 0), iota((EP, 128), 1)
        source = c % 64 * (8 * lm_count) + info_ref[3]
        hit = (r == source) & (c % 64 < n2)
        at0 = (hit & (c < 64)).astype(bf16)
        at1 = (hit & (c >= 64)).astype(bf16)
        return spread_lanes(at0, low) + spread_lanes(at1, up)

    got = both_halves(a2[0, 0:E, EP : 2 * EP], a2[0, 0:E, 2 * EP : 3 * EP])
    fac_ref[1, :, n0 + n1 : n0 + n1 + n2] = got[:, 0:n2]
    fac_ref[2, :, n0 + n1 : n0 + n1 + n2] = got[:, 64 : 64 + n2]
    part = minus_rows(got.T, a2[0, 0:E, EP : 3 * EP])
    rows0 = both_halves(odd_up[0], odd_up[1]).T
    rows1 = both_halves(a1[0, 0:E, 2 * EP : 3 * EP], a1[1, 0:E, 2 * EP : 3 * EP]).T
    for h in range(2):
        own = minus_rows(rows0[64 * h : 64 * h + 64], odd_up[h])
        own = own + minus_rows(rows1[64 * h : 64 * h + 64], a1[h, 0:E, 2 * EP : 3 * EP])
        mine = pl.ds(info_ref[3], n2, stride=8 * lm_count)
        kept = [pri[h * (EP // 128) + v, mine, :] for v in range(EP // 128)]
        own = own[0:n2] + jnp.concatenate(kept, axis=1)
        for g in range(2):
            value = part[64 * h : 64 * h + n2, g * EP : g * EP + EP]
            if g == h:
                value = value + own
            top_ref[h, :, 0, g * E : g * E + E] = value[:, 0:E]


def vmem(n):
    return [pl.BlockSpec(memory_space=pltpu.VMEM)] * n


def smem(n):
    return [pl.BlockSpec(memory_space=pltpu.SMEM)] * n


LIMIT = 60 * 1024 * 1024


def local(jacobian, camera_block, landmark_block):
    lm_count = lax.axis_size("lm")
    sub_count = lax.axis_size("sub")
    lm_place = lax.axis_index("lm")
    sub_place = lax.axis_index("sub")
    group = 2**LEVELS
    jac = jacobian[0]
    blocks = jac.shape[0]

    def swap(value, sub_mask, lm_mask):
        pairs = [
            (s * lm_count + l, (s ^ sub_mask) * lm_count + (l ^ lm_mask))
            for s in range(sub_count)
            for l in range(lm_count)
        ]
        return lax.ppermute(value, ("sub", "lm"), pairs)

    info = jnp.stack(
        [
            sub_place % group,
            sub_place % 2 * lm_count + lm_place,
            sub_place % 4 * lm_count + lm_place,
            sub_place % 8 * lm_count + lm_place,
            jnp.int32(2 * lm_count),
            lm_place,
        ]
    ).astype(jnp.int32)
    cams = camera_block[0]
    lms = landmark_block[0] - NB
    payload = jax.ShapeDtypeStruct((48 * blocks + 8, 128), f32)

    pay, sums = pl.pallas_call(
        tiles_kernel,
        out_shape=(payload, jax.ShapeDtypeStruct(((NB + 1) // 2 * 64, 128), f32)),
        in_specs=smem(2) + vmem(1),
        out_specs=tuple(vmem(2)),
    )(cams, lms, jac)
    half_sums = sums + swap(sums, 1, 0)
    other_sums = swap(half_sums, 0, 1)

    count0 = E // (2 * lm_count)
    pay, own0 = pl.pallas_call(
        bottom_kernel,
        out_shape=(payload, jax.ShapeDtypeStruct((E, count0), f32)),
        in_specs=smem(2) + vmem(3),
        out_specs=tuple(vmem(2)),
        scratch_shapes=[pltpu.VMEM((NB, 64, 192), bf16), pltpu.VMEM((NB, 64, 128), f32)],
    )(info, cams, half_sums, other_sums, pay)

    held = {(0, 0): pay}
    for sub_mask, lm_mask in ((0, 1), (2, 0), (4, 0), (1, 0)):
        held.update({(q ^ sub_mask, l ^ lm_mask): swap(v, sub_mask, lm_mask) for (q, l), v in held.items()})
    slots = [held[q, l] for q in range(group) for l in range(2)]
    nslots = len(slots)
    per = blocks * 2
    factors, top = pl.pallas_call(
        functools.partial(upper_kernel, nslots, blocks, lm_count),
        out_shape=(
            jax.ShapeDtypeStruct((3, E, count0 * 7 // 4), f32),
            jax.ShapeDtypeStruct((2, count0 // 4, 1, F), f32),
        ),
        in_specs=smem(1) + vmem(nslots + 1),
        out_specs=tuple(vmem(2)),
        scratch_shapes=[
            pltpu.VMEM((nslots * blocks * 64, 128), f32),
            pltpu.VMEM((nslots * 8, 128), jnp.int32),
            pltpu.SMEM((nslots * 8, 128), jnp.int32),
            pltpu.SemaphoreType.DMA(()),
            pltpu.VMEM((4, 64, 2 * per * 128), f32),
            pltpu.VMEM((per * 64, 2 * per * 128), f32),
            pltpu.VMEM((per * 64, 192), bf16),
            pltpu.VMEM((E, 2 * EP), f32),
            pltpu.VMEM((2, E, EP), f32),
            pltpu.VMEM((2, EP, 3 * EP), f32),
            pltpu.VMEM((1, EP, 3 * EP), f32),
            pltpu.VMEM((2 * (EP // 128), E, 128), f32),
            pltpu.VMEM((2, 64, 192), bf16),
            pltpu.VMEM((2, 128, 192), bf16),
            pltpu.VMEM((2, EP, 192), bf16),
            pltpu.VMEM((2, 192, 3 * EP), bf16),
            pltpu.VMEM((EP, 3 * EP), bf16),
            pltpu.VMEM((3 * EP, 2 * EP), bf16),
        ],
        compiler_params=pltpu.CompilerParams(vmem_limit_bytes=LIMIT),
    )(info, *slots, own0)
    return jnp.transpose(factors, (0, 2, 1))[:, None], jnp.transpose(top, (0, 2, 1, 3))


def solution(mesh):
    placed = (P("sub", "lm", None, None), P("sub", "lm"), P("sub", "lm"))
    return jax.shard_map(
        local,
        mesh=mesh,
        in_specs=placed,
        out_specs=(P(None, ("sub", "lm"), None, None), P(None, ("sub", "lm"), None, None)),
        check_vma=False,
    )
```

```python
import functools

import jax
import jax.numpy as jnp
from jax import lax
from jax.experimental import pallas as pl
from jax.experimental.pallas import tpu as pltpu
from jax.sharding import PartitionSpec as P

BW = 64
F = 1152
LEVELS = 3
E = 576
NB = E // BW
EP = 640
DAMPING = 1.0
f32 = jnp.float32
bf16 = jnp.bfloat16


def iota(shape, axis):
    return lax.broadcasted_iota(jnp.int32, shape, axis)


def row_of(x, t):
    return jnp.broadcast_to(x[t : t + 1, :], x.shape)


def col_of(x, j):
    return jnp.broadcast_to(x[:, j : j + 1], x.shape)


def split2(x):
    hi = x.astype(bf16)
    return hi, (x - hi.astype(f32)).astype(bf16)


def left3(dup):
    hi, lo = split2(dup)
    return jnp.concatenate([hi, lo[:, :64]], axis=1)


def right3(x):
    hi, lo = split2(x)
    return jnp.concatenate([hi, lo, hi], axis=0)


def dot(a, b):
    return jnp.dot(a, b, preferred_element_type=f32)


def dot_nt(a, b):
    return lax.dot_general(a, b, (((1,), (1,)), ((), ())), preferred_element_type=f32)


def roll64(x):
    return pltpu.roll(x, 64, 1)


def factor(mats):
    sub = iota((8, 128), 0)
    zero = [m[0] - m[0] for m in mats]

    def spread(b, x, kb):
        return [col_of(x, 8 * kb + t) + zero[b] for t in range(8)]

    ready = [spread(b, m[0], 0) for b, m in enumerate(mats)]
    for kb in range(8):
        state, below = [], []
        for b, m in enumerate(mats):
            parts = [spread(b, m[v], kb) if v == kb + 1 else [col_of(m[v], 8 * kb + t) for t in range(8)] for v in range(kb + 1, 8)]
            below.append(parts)
            coming = spread(b, m[kb + 1], kb + 1) if kb < 7 else []
            ahead = list(parts[0]) if kb < 7 else []
            state.append([m[kb], m[kb], ready[b], jnp.ones((8, 128), f32), jnp.ones((8, 128), f32), ahead, coming])
        for t in range(8):
            for st in state:
                fwd, both, cols, diag, recip, ahead, coming = st
                col = cols[t]
                d = row_of(col, t)
                rd = 1.0 / d
                st[3] = jnp.where(sub == t, d, diag)
                st[4] = jnp.where(sub == t, rd, recip)
                mult = jnp.where(sub == t, 0.0, col * rd)
                for t2 in range(t + 1, 8):
                    cols[t2] = cols[t2] - mult * row_of(cols[t2], t)
                st[1] = both - mult * row_of(both, t)
                st[0] = fwd - jnp.where(sub > t, mult, 0.0) * row_of(fwd, t)
                if ahead:
                    weight = ahead[t]
                    scaled = weight * rd
                    for t2 in range(t + 1, 8):
                        ahead[t2] = ahead[t2] - scaled * row_of(col, t2)
                    for t2 in range(8):
                        coming[t2] = coming[t2] - weight * row_of(scaled, t2)
        for b, m in enumerate(mats):
            fwd, both, cols, diag, recip, ahead, coming = state[b]
            m[kb] = fwd * lax.rsqrt(diag)
            solved = both * recip
            rows = [row_of(solved, t) for t in range(8)]
            for v in range(kb + 1, 8):
                terms = [below[b][v - kb - 1][t] * rows[t] for t in range(8)]
                while len(terms) > 1:
                    terms = [x + y for x, y in zip(terms[0::2], terms[1::2])]
                m[v] = m[v] - terms[0]
            ready[b] = coming
    return mats


def augmented(x):
    lane, row = iota((64, 128), 1), iota((64, 128), 0)
    full = jnp.where(lane < 64, x, jnp.where(lane - 64 == row, 1.0, 0.0))
    return [full[8 * v : 8 * v + 8] for v in range(8)]


def joined(rows):
    return jnp.concatenate(rows, axis=0)


def tiles_kernel(cam_ref, lm_ref, jac_ref, pay_ref, sum_ref):
    lane = iota((64, 128), 1)
    blocks = jac_ref.shape[0]
    sum_ref[...] = jnp.zeros_like(sum_ref)
    lane8, row8 = iota((8, 128), 1), iota((8, 128), 0)
    row, col = iota((64, 128), 0), lane % 64
    index = jnp.zeros((8, 128), f32)
    tops, lls = [], []
    for n in range(blocks):
        j = jac_ref[n]
        t = lax.dot_general(j, j, (((0,), (0,)), ((), ())), preferred_element_type=f32)
        top = t[:64]
        tops.append(top)
        lls.append(t[64:])
        c = cam_ref[n]
        cc = jnp.where(lane < 64, top, roll64(top))
        mine = (lane >= 64).astype(jnp.int32) == c % 2
        at = pl.ds(pl.multiple_of(c // 2 * 64, 64), 64)
        sum_ref[at, :] = sum_ref[at, :] + jnp.where(mine, cc, 0.0)
        index = jnp.where((lane8 == n) & (row8 == 0), c.astype(f32), index)
        index = jnp.where((lane8 == n) & (row8 == 1), (lm_ref[n] - NB).astype(f32), index)
    for k in range(blocks // 2):
        both = jnp.where(lane < 64, roll64(tops[2 * k]), tops[2 * k + 1])
        pay_ref[64 * k : 64 * k + 64, :] = both
    for k in range(blocks // 4):
        first = jnp.where(lane < 64, roll64(lls[4 * k]), lls[4 * k + 2])
        second = jnp.where(lane < 64, roll64(lls[4 * k + 1]), lls[4 * k + 3])
        base = 64 * (blocks // 2 + k)
        pay_ref[base : base + 64, :] = jnp.where(row >= col, first, second)
        diag = jnp.sum(jnp.where(row == col, second, 0.0), axis=0, keepdims=True)
        index = jnp.where(row8 == 2 + k, jnp.broadcast_to(diag, (8, 128)), index)
    pay_ref[64 * (3 * blocks // 4) :, :] = index


def bottom_kernel(info_ref, cam_ref, sum_a, sum_b, pay_ref, out_ref, own_ref, w_ref, v_ref):
    lane, row = iota((64, 128), 1), iota((64, 128), 0)
    own_ref[...] = jnp.zeros_like(own_ref)
    together = 3

    def several(g, carry):
        mats = []
        for i in range(together):
            c = g * together + i
            at = pl.ds(pl.multiple_of(c // 2 * 64, 64), 64)
            x = sum_a[at, :] + sum_b[at, :]
            x = jnp.where(c % 2 == 1, roll64(x), x)
            mats.append(augmented(x + jnp.where(lane == row, 2 * DAMPING, 0.0)))
        mats = factor(mats)
        for i in range(together):
            v_ref[g * together + i] = joined(mats[i])
        return carry

    lax.fori_loop(0, NB // together, several, 0)
    spread = info_ref[4]
    place = info_ref[1]
    count = own_ref.shape[1] // NB
    pick = (iota((128, count), 0) == iota((128, count), 1) * spread + place).astype(bf16)
    for c in range(NB):
        v = v_ref[c]
        w = roll64(v)
        w_ref[c] = left3(jnp.where(lane < 64, w, v))
        upper = jnp.where((lane >= row) & (lane < 64), v, 0.0)
        hi, lo = split2(upper)
        own_ref[64 * c : 64 * c + 64, count * c : count * c + count] = dot(hi, pick) + dot(lo, pick)
    blocks = cam_ref.shape[0]
    for k in range(blocks // 2):
        x = pay_ref[64 * k : 64 * k + 64, :]
        xr = roll64(x)
        y0 = dot(w_ref[cam_ref[2 * k]], right3(jnp.where(lane < 64, x, xr)))
        y1 = dot(w_ref[cam_ref[2 * k + 1]], right3(jnp.where(lane < 64, xr, x)))
        out_ref[64 * k : 64 * k + 64, :] = jnp.where(lane < 64, y0, y1)
    out_ref[32 * blocks :, :] = pay_ref[32 * blocks :, :]


def climb(a_ref, w_ref, n_ref, l_ref, r_ref, batch):
    lane64 = iota((64, 128), 1)
    width = a_ref.shape[2]

    def keep_inverse(b, mat):
        v = joined(mat)
        hi, lo = split2(jnp.where(lane64 < 64, roll64(v), v))
        w_ref[b] = jnp.concatenate([hi, lo[:, :64]], axis=1)
        n = jnp.concatenate([jnp.where(lane64 < 64, hi, lo), hi[:, :64]], axis=1)
        n_ref[b] = jnp.concatenate([n, n], axis=0)

    def finish(b, w, at, j):
        u = dot(w, right3(a_ref[b, at, :]))
        keep = iota((64, EP), 1) >= j * 64 + iota((64, EP), 0)
        us = jnp.where(keep, u[:, :EP], 0.0)
        a_ref[b, at, 0:EP] = us
        a_ref[b, at, EP:] = u[:, EP:]
        return us, u

    mats = factor([augmented(a_ref[b, 0:64, 0:128]) for b in range(batch)])
    for b in range(batch):
        keep_inverse(b, mats[b])

    for first, last in ((1, 4), (4, 7), (7, 9)):
        low_row = 64 * first
        low_lane = low_row // 128 * 128
        starts = [low_lane] + list(range(EP, width, EP))
        sizes = [EP - low_lane] + [EP] * (len(starts) - 1)

        def step(j, carry, low_row=low_row, starts=starts, sizes=sizes):
            at = pl.ds(pl.multiple_of(j * 64 - 64, 64), 64)
            rows = pl.ds(pl.multiple_of(j * 64, 64), 64)
            wide = pl.ds(pl.multiple_of(j // 2 * 128, 128), 128)
            narrow = pl.ds(pl.multiple_of((j - 1) // 2 * 128, 128), 128)
            odd = j % 2 == 1
            olds = [w_ref[b] for b in range(batch)]
            mats = []
            for b in range(batch):
                us = dot(olds[b], right3(a_ref[b, at, wide]))
                us = jnp.where(odd, roll64(us), us)
                side = a_ref[b, rows, narrow]
                turned = roll64(side)
                side = jnp.where((lane64 < 64) == odd, side, turned)
                left = left3(-dot_nt(left3(side), n_ref[b]))
                x = a_ref[b, rows, wide]
                x = jnp.where(odd, roll64(x), x)
                mats.append(augmented(x + dot(left, right3(us))))
            mats = factor(mats)
            for b in range(batch):
                us, u = finish(b, olds[b], at, j - 1)
                xs = jnp.where(iota((64, EP), 1) >= j * 64, -us, 0.0)
                l_ref[b] = left3(jnp.concatenate([xs, xs], axis=0).T)
                r_ref[b] = right3(u)
                left = l_ref[b, low_row:E]
                for s, size in zip(starts, sizes):
                    a_ref[b, low_row:E, s : s + size] = a_ref[b, low_row:E, s : s + size] + dot(
                        left, r_ref[b, :, s : s + size]
                    )
            for b in range(batch):
                keep_inverse(b, mats[b])
            return carry

        lax.fori_loop(first, last, step, 0)
    for b in range(batch):
        finish(b, w_ref[b], slice(E - 64, E), NB - 1)


def gram_left(u, left_ref):
    hi, lo = split2((-u).T)
    left_ref[:, 0:EP] = hi
    left_ref[:, EP : 2 * EP] = hi
    left_ref[:, 2 * EP :] = lo


def spread_lanes(pick, u):
    hi, lo = split2(u)
    return dot(hi, pick) + dot(lo, pick)


def minus_rows(rows, u):
    count = rows.shape[0]
    hi, lo = split2(-rows)
    uh, ul = split2(u)
    both = dot(jnp.concatenate([hi, lo], axis=0), uh)
    return both[:count] + both[count:] + dot(hi, ul)


def upper_kernel(nslots, blocks, lm_count_static, info_ref, *refs):
    pays = refs[:nslots]
    own0_ref, fac_ref, top_ref = refs[nslots : nslots + 3]
    (all_ref, ivm, ism, sem, ydup, tbuf, lbuf, own_u0, odd_up, a1, a2, pri) = refs[nslots + 3 : nslots + 15]
    (w_ref, n_ref, l_ref, r_ref, left_ref, right_ref) = refs[nslots + 15 :]
    lane, row = iota((64, 128), 1), iota((64, 128), 0)
    col = lane % 64
    me, my_lm = info_ref[0], info_ref[5]
    lm_count = lm_count_static
    per = blocks * nslots // 8

    for slot in range(nslots):
        s = me ^ (slot // 2)
        spot = s * 2 + (my_lm ^ (slot % 2))
        tail = pays[slot][48 * blocks : 48 * blocks + 8, :]
        ivm[pl.ds(pl.multiple_of(spot * 8, 8), 8), :] = tail.astype(jnp.int32)
        for k in range(blocks // 4):
            base = 64 * (blocks // 2 + k)
            packed = pays[slot][base : base + 64, :]
            turned = jnp.concatenate([packed, packed], axis=0).T
            turned = jnp.where(lane < 64, turned[0:64], turned[64:128])
            diag = jnp.broadcast_to(tail[2 + k : 3 + k, :], (64, 128))
            first = jnp.where(row >= col, packed, turned)
            second = jnp.where(row < col, packed, jnp.where(row > col, turned, diag))
            for i in range(2):
                y = pays[slot][64 * (2 * k + i) : 64 * (2 * k + i) + 64, :]
                yr = roll64(y)
                for h, ll in enumerate((first, second)):
                    at = pl.ds(pl.multiple_of((spot * blocks + 4 * k + 2 * i + h) * 64, 64), 64)
                    ll = ll if i else roll64(ll)
                    all_ref[at, :] = jnp.where(lane < 64, yr if h else y, ll)
    copy = pltpu.make_async_copy(ivm, ism, sem)
    copy.start()
    eye2 = jnp.where(iota((E, EP), 0) == iota((E, EP), 1), 2 * DAMPING, 0.0)
    own_u0[...] = jnp.zeros_like(own_u0)
    odd_up[...] = jnp.zeros_like(odd_up)
    for m in range(2):
        a1[m] = jnp.zeros(a1.shape[1:], f32)
        a1[m, 0:E, 0:EP] = eye2
        for v in range(EP // 128):
            pri[m * (EP // 128) + v] = 0.5 * eye2[:, 128 * v : 128 * v + 128]
    a2[0, 0:E, 0:EP] = eye2
    copy.wait()

    def ids(s, k):
        row = (s * 2 + k // blocks) * 8
        return ism[row, k % blocks], ism[row + 1, k % blocks]

    def rows64(i):
        return pl.ds(pl.multiple_of(i * 64, 64), 64)

    def lanes128(i):
        return pl.ds(pl.multiple_of(i * 128, 128), 128)

    def dups(s, k):
        x = all_ref[rows64(s * per + k), :]
        xr = roll64(x)
        return jnp.where(lane < 64, x, xr), jnp.where(lane < 64, xr, x)

    def half_of(l):
        return (lane >= 64).astype(jnp.int32) == l % 2

    for s in range(8):
        pair, half, merge = s // 2, s % 2, s // 4
        second = pair % 2

        def place(k, carry, s=s, pair=pair, half=half, merge=merge, second=second):
            c, l = ids(s, k)
            y, ll = dups(s, k)
            mine = half_of(l)
            ydup[pair, :, lanes128(half * per + k)] = y
            rows, lanes = rows64(l), lanes128(l // 2)
            ll = jnp.where(mine, ll, 0.0)
            if half == 0:
                a1[merge, rows, lanes] = a1[merge, rows, lanes] + ll
            elif second == 0:
                a2[0, rows, lanes] = a2[0, rows, lanes] + ll
            else:
                tile = merge * (EP // 128) + l // 2
                pri[tile, rows, :] = pri[tile, rows, :] + ll
                odd_up[merge, rows64(c), lanes] = odd_up[merge, rows64(c), lanes] + jnp.where(mine, y, 0.0)
            return carry

        lax.fori_loop(0, per, place, 0)

    my_pair = me // 2
    for half in range(2):

        def place_own(k, carry, half=half):
            c, l = ids(2 * my_pair + half, k)
            y, _ = dups(2 * my_pair + half, k)
            lanes = lanes128(half * (EP // 128) + l // 2)
            own_u0[rows64(c), lanes] = own_u0[rows64(c), lanes] + jnp.where(half_of(l), y, 0.0)
            return carry

        lax.fori_loop(0, per, place_own, 0)

    def gram_pair(p, carry):
        merge = p // 2

        def transposed(first):
            for k in range(per):
                t = ydup[p, :, 128 * (first + k) : 128 * (first + k + 1)]
                tt = jnp.concatenate([t, t], axis=0).T
                lbuf[64 * k : 64 * k + 64, :] = left3(-tt[0:64])

        def scatter(target, s_rows, halves, base):
            def body(n, carry):
                cn, ln = ids(s_rows, n)
                for i, h in enumerate(halves):
                    for k in range(per):
                        ck, lk = ids(2 * p + h, k)

                        @pl.when(ck == cn)
                        def _():
                            got = tbuf[rows64(n), 128 * (i * per + k) : 128 * (i * per + k + 1)]
                            to = pl.ds(pl.multiple_of(base[h] + lk // 2 * 128, 128), 128)
                            view = target.at[rows64(ln), to]
                            view[...] = view[...] + jnp.where(half_of(lk), got, 0.0)

                return carry

            lax.fori_loop(0, per, body, 0)

        transposed(0)
        wide = 128 * per
        for h in range(2):
            tbuf[:, h * wide : h * wide + wide] = dot(lbuf[...], right3(ydup[p, :, h * wide : h * wide + wide]))
        scatter(a1.at[merge], 2 * p, (0, 1), (0, EP + p % 2 * EP))

        @pl.when(p % 2 == 0)
        def _():
            transposed(per)
            tbuf[:, 0:wide] = dot(lbuf[...], right3(ydup[p, :, wide : 2 * wide]))
            scatter(a2.at[0], 2 * p + 1, (1,), (0, 0))

        return carry

    lax.fori_loop(0, 4, gram_pair, 0)

    climb(a1, w_ref, n_ref, l_ref, r_ref, 2)

    def gram_merge(m, carry):
        u = a1[m, :, EP : 3 * EP]
        hi, lo = split2(u)
        right_ref[0:EP] = hi
        right_ref[EP : 2 * EP] = lo
        right_ref[2 * EP :] = hi
        gram_left(u[:, 0:EP], left_ref)
        a2[0, 0:E, 0:EP] = a2[0, 0:E, 0:EP] + dot(left_ref[0:E], right_ref[:, 0:EP])
        to = pl.ds(pl.multiple_of(EP + m * EP, 128), EP)
        a2[0, 0:E, to] = dot(left_ref[0:E], right_ref[:, EP : 2 * EP])
        return carry

    lax.fori_loop(0, 2, gram_merge, 0)

    climb(a2, w_ref, n_ref, l_ref, r_ref, 1)

    def pick_of(count, spread, place):
        return (iota((EP, count), 0) == iota((EP, count), 1) * spread + place).astype(bf16)

    n0 = own0_ref.shape[1]
    n1, n2 = n0 // 2, n0 // 4
    merge = me // 4
    pick0 = pick_of(n0, 2 * lm_count, info_ref[1])
    pick1 = pick_of(n1, 4 * lm_count, info_ref[2])
    pick2 = pick_of(n2, 8 * lm_count, info_ref[3])
    fac_ref[0, :, 0:n0] = own0_ref[...]
    fac_ref[1, :, 0:n0] = spread_lanes(pick0, own_u0[:, 0:EP])
    fac_ref[2, :, 0:n0] = spread_lanes(pick0, own_u0[:, EP : 2 * EP])
    for t in range(3):
        fac_ref[t, :, n0 : n0 + n1] = spread_lanes(pick1, a1[merge, 0:E, t * EP : t * EP + EP])
    fac_ref[0, :, n0 + n1 : n0 + n1 + n2] = spread_lanes(pick2, a2[0, 0:E, 0:EP])

    def both_halves(low, up):
        r, c = iota((EP, 128), 0), iota((EP, 128), 1)
        source = c % 64 * (8 * lm_count) + info_ref[3]
        hit = (r == source) & (c % 64 < n2)
        at0 = (hit & (c < 64)).astype(bf16)
        at1 = (hit & (c >= 64)).astype(bf16)
        return spread_lanes(at0, low) + spread_lanes(at1, up)

    got = both_halves(a2[0, 0:E, EP : 2 * EP], a2[0, 0:E, 2 * EP : 3 * EP])
    fac_ref[1, :, n0 + n1 : n0 + n1 + n2] = got[:, 0:n2]
    fac_ref[2, :, n0 + n1 : n0 + n1 + n2] = got[:, 64 : 64 + n2]
    part = minus_rows(got.T, a2[0, 0:E, EP : 3 * EP])
    rows0 = both_halves(odd_up[0], odd_up[1]).T
    rows1 = both_halves(a1[0, 0:E, 2 * EP : 3 * EP], a1[1, 0:E, 2 * EP : 3 * EP]).T
    for h in range(2):
        own = minus_rows(rows0[64 * h : 64 * h + 64], odd_up[h])
        own = own + minus_rows(rows1[64 * h : 64 * h + 64], a1[h, 0:E, 2 * EP : 3 * EP])
        mine = pl.ds(info_ref[3], n2, stride=8 * lm_count)
        kept = [pri[h * (EP // 128) + v, mine, :] for v in range(EP // 128)]
        own = own[0:n2] + jnp.concatenate(kept, axis=1)
        for g in range(2):
            value = part[64 * h : 64 * h + n2, g * EP : g * EP + EP]
            if g == h:
                value = value + own
            top_ref[h, :, 0, g * E : g * E + E] = value[:, 0:E]


def vmem(n):
    return [pl.BlockSpec(memory_space=pltpu.VMEM)] * n


def smem(n):
    return [pl.BlockSpec(memory_space=pltpu.SMEM)] * n


LIMIT = 60 * 1024 * 1024


def local(jacobian, camera_block, landmark_block):
    lm_count = lax.axis_size("lm")
    sub_count = lax.axis_size("sub")
    lm_place = lax.axis_index("lm")
    sub_place = lax.axis_index("sub")
    group = 2**LEVELS
    jac = jacobian[0]
    blocks = jac.shape[0]

    def swap(value, sub_mask, lm_mask):
        pairs = [
            (s * lm_count + l, (s ^ sub_mask) * lm_count + (l ^ lm_mask))
            for s in range(sub_count)
            for l in range(lm_count)
        ]
        return lax.ppermute(value, ("sub", "lm"), pairs)

    info = jnp.stack(
        [
            sub_place % group,
            sub_place % 2 * lm_count + lm_place,
            sub_place % 4 * lm_count + lm_place,
            sub_place % 8 * lm_count + lm_place,
            jnp.int32(2 * lm_count),
            lm_place,
        ]
    ).astype(jnp.int32)
    cams = camera_block[0]
    lms = landmark_block[0]
    payload = jax.ShapeDtypeStruct((48 * blocks + 8, 128), f32)

    pay, sums = pl.pallas_call(
        tiles_kernel,
        out_shape=(payload, jax.ShapeDtypeStruct(((NB + 1) // 2 * 64, 128), f32)),
        in_specs=smem(2) + vmem(1),
        out_specs=tuple(vmem(2)),
    )(cams, lms, jac)
    half_sums = sums + swap(sums, 1, 0)
    other_sums = swap(half_sums, 0, 1)

    count0 = E // (2 * lm_count)
    pay, own0 = pl.pallas_call(
        bottom_kernel,
        out_shape=(payload, jax.ShapeDtypeStruct((E, count0), f32)),
        in_specs=smem(2) + vmem(3),
        out_specs=tuple(vmem(2)),
        scratch_shapes=[pltpu.VMEM((NB, 64, 192), bf16), pltpu.VMEM((NB, 64, 128), f32)],
    )(info, cams, half_sums, other_sums, pay)

    held = {(0, 0): pay}
    for sub_mask, lm_mask in ((0, 1), (2, 0), (4, 0), (1, 0)):
        held.update({(q ^ sub_mask, l ^ lm_mask): swap(v, sub_mask, lm_mask) for (q, l), v in held.items()})
    slots = [held[q, l] for q in range(group) for l in range(2)]
    nslots = len(slots)
    per = blocks * 2
    factors, top = pl.pallas_call(
        functools.partial(upper_kernel, nslots, blocks, lm_count),
        out_shape=(
            jax.ShapeDtypeStruct((3, E, count0 * 7 // 4), f32),
            jax.ShapeDtypeStruct((2, count0 // 4, 1, F), f32),
        ),
        in_specs=smem(1) + vmem(nslots + 1),
        out_specs=tuple(vmem(2)),
        scratch_shapes=[
            pltpu.VMEM((nslots * blocks * 64, 128), f32),
            pltpu.VMEM((nslots * 8, 128), jnp.int32),
            pltpu.SMEM((nslots * 8, 128), jnp.int32),
            pltpu.SemaphoreType.DMA(()),
            pltpu.VMEM((4, 64, 2 * per * 128), f32),
            pltpu.VMEM((per * 64, 2 * per * 128), f32),
            pltpu.VMEM((per * 64, 192), bf16),
            pltpu.VMEM((E, 2 * EP), f32),
            pltpu.VMEM((2, E, EP), f32),
            pltpu.VMEM((2, EP, 3 * EP), f32),
            pltpu.VMEM((1, EP, 3 * EP), f32),
            pltpu.VMEM((2 * (EP // 128), E, 128), f32),
            pltpu.VMEM((2, 64, 192), bf16),
            pltpu.VMEM((2, 128, 192), bf16),
            pltpu.VMEM((2, EP, 192), bf16),
            pltpu.VMEM((2, 192, 3 * EP), bf16),
            pltpu.VMEM((EP, 3 * EP), bf16),
            pltpu.VMEM((3 * EP, 2 * EP), bf16),
        ],
        compiler_params=pltpu.CompilerParams(vmem_limit_bytes=LIMIT),
    )(info, *slots, own0)
    return jnp.transpose(factors, (0, 2, 1))[:, None], jnp.transpose(top, (0, 2, 1, 3))


def solution(mesh):
    placed = (P("sub", "lm", None, None), P("sub", "lm"), P("sub", "lm"))
    return jax.shard_map(
        local,
        mesh=mesh,
        in_specs=placed,
        out_specs=(P(None, ("sub", "lm"), None, None), P(None, ("sub", "lm"), None, None)),
        check_vma=False,
    )
```
